512 devices in a mesh: row: 64 (over y, x, core), col: 8 (over z).
Axes of the slice: x: 4, y: 8, z: 8, core: 2. Of those that a mesh axis runs over, the one named last changes fastest.
Arguments:
- near_blocks: float32 [512, 8, 256, 256], P('row', 'col'), may hold values from -0.125 to 0.125
- column_block: int32 [512, 8], P('row', 'col'), may hold values from 0 to 511, as said below
- test_panels: float32 [512, 256, 256], P(('row', 'col')), may hold values from -6 to 6
- nugget: float32 [512, 256], P('row'), may hold values from 0.5 to 2
Outputs:
- leaf_basis: float32 [512, 128, 256], P('row', None, 'col')
- leaf_miss: float32 [512, 128, 256], P('row', None, 'col')
- local_basis: float32 [448, 128, 256], P('row', None, 'col')
- upper_basis: float32 [64, 128, 256], P('row', None, 'col')
The draws below stay inside these ranges and needn't reach their ends.
Inputs may be any that keep to these rules, and one draw needn't show every extreme that they name: `column_block`: row i names 8 different leaf blocks, i itself among them, all within i - 8 to i + 8.
All inputs are finite; a program needn't handle non-finite values.
Results may differ from the reference program's by a relative error of at most 0.0003.
Values sent between devices are 32-bit elements; how exact they have to be, the bound alone decides.
No kernel may reach another device: no remote copies, remote signals or barrier semaphores. Data moves between devices by JAX's collectives and lax.ppermute only.
A program may use at most 64 MiB of HBM per device.

```python
import math
import jax
import jax.numpy as jnp
import numpy as np
from jax import lax

BLOCK = 256
PANEL = 128
LEAF_DEV = 8
NEAR = 8
LEAVES = 512
LEVELS_UP = 6
N_ROW = 64


def draw_column_block(key, part):
    window = 2 * LEAF_DEV + 1
    leaf_index = jnp.arange(LEAVES, dtype=jnp.int32)[:, None]
    offsets = jnp.arange(window, dtype=jnp.int32)[None, :] - LEAF_DEV
    target = leaf_index + offsets
    valid = (target >= 0) & (target < LEAVES)
    first_key = jax.random.fold_in(key, 11)
    second_key = jax.random.fold_in(key, 23)
    noise = jax.random.randint(first_key, (LEAVES, window), 0, 1 << 20)
    scores = noise * window + jnp.arange(window, dtype=jnp.int32)[None, :]
    scores = jnp.where(valid, scores, -1)
    scores = jnp.where(offsets == 0, (1 << 20) * window + window, scores)
    chosen_scores, chosen = lax.top_k(scores, NEAR)
    picked = jnp.take_along_axis(target, chosen, axis=1)
    shuffle = jax.random.randint(second_key, (LEAVES, NEAR), 0, 1 << 20) * NEAR + jnp.arange(NEAR, dtype=jnp.int32)[None, :]
    order_scores, order = lax.top_k(shuffle, NEAR)
    return jnp.take_along_axis(picked, order, axis=1).astype(jnp.int32)


def draw_test_panels(key, part):
    base_key = jax.random.fold_in(key, 31)
    sign_key = jax.random.fold_in(key, 37)
    column_key = jax.random.fold_in(key, 41)
    shape = (LEAVES, BLOCK, 2 * PANEL)
    base = jax.random.normal(base_key, shape, jnp.float32)
    signs = jax.random.randint(sign_key, (LEAVES, BLOCK, 1), 0, 2).astype(jnp.float32) * 2.0 - 1.0
    shared = jax.random.normal(column_key, (1, 1, 2 * PANEL), jnp.float32)
    return jnp.clip(base + signs * shared, -6.0, 6.0).astype(jnp.float32)


def shard_levels(stream_key, shape, shards, least, top_value):
    def one(axis_at, blocks):
        draws = jax.random.uniform(jax.random.fold_in(jax.random.fold_in(stream_key, 6), axis_at), (blocks,), jnp.float32, least / len(shards), top_value / len(shards))
        return jnp.repeat(jnp.exp(draws), shape[axis_at] // blocks).reshape((-1,) + (1,) * (len(shape) - axis_at - 1))

    level = one(*shards[0])
    for cut in shards[1:]:
        level = level * one(*cut)
    return level


def bell_draw(key, extent, deviation, bound, split=(), held_as=jnp.bfloat16):
    entries = jax.random.normal(key, extent, jnp.float32) * deviation
    if len(split) > 0:
        entries = shard_levels(key, extent, split, -0.22, 0.18) * entries
    return jnp.clip(entries, min=-bound, max=bound).astype(held_as)


def setup_inputs(seed: int = 0) -> dict:
    seeds = jax.random.split(jax.random.key(seed), 5)
    return {
        "near_blocks": bell_draw(seeds[0], (LEAVES, NEAR, BLOCK, BLOCK), (BLOCK * NEAR) ** -0.5, 0.125, ((0, 64), (1, 8)), jnp.float32),
        "column_block": draw_column_block(jax.random.fold_in(seeds[4], 71), 0),
        "test_panels": draw_test_panels(jax.random.fold_in(seeds[4], 71), 0),
        "nugget": jnp.clip(jnp.exp(math.log(2.0) - 1.3862944 * jax.random.uniform(seeds[3], (LEAVES, BLOCK), jnp.float32) ** shard_levels(seeds[3], (LEAVES, BLOCK), ((0, 64),), -0.2, 0.2)), 0.5, 2.0),
    }


def product(left, right):
    return jnp.matmul(left, right, precision=lax.Precision.HIGHEST)

def combine(factor_a, panel_a, factor_b, panel_b):
    gram_matrix = product(factor_a, jnp.swapaxes(factor_a, -1, -2)) + product(factor_b, jnp.swapaxes(factor_b, -1, -2))
    factor = jnp.linalg.cholesky(gram_matrix)
    basis_node = jax.scipy.linalg.solve_triangular(factor, jnp.concatenate([factor_a, factor_b], axis=-1), lower=True)
    reduced = jax.scipy.linalg.solve_triangular(factor, product(factor_a, panel_a) + product(factor_b, panel_b), lower=True)
    return (basis_node, factor, reduced)

def reference(near_blocks, column_block, test_panels, nugget):

    def one_leaf(leaf_index):
        blocks = near_blocks[leaf_index]
        picked = jnp.take(test_panels, column_block[leaf_index], axis=0)
        total = jnp.einsum('kab,kbs->as', blocks, picked, precision=lax.Precision.HIGHEST)
        return total + nugget[leaf_index][:, None] * test_panels[leaf_index]
    sample = lax.map(one_leaf, jnp.arange(LEAVES, dtype=jnp.int32))
    panel_one = sample[:, :, :PANEL]
    panel_two = sample[:, :, PANEL:]
    gram_matrix = jnp.einsum('las,lat->lst', panel_one, panel_one, precision=lax.Precision.HIGHEST)
    cross_gram = jnp.einsum('las,lat->lst', panel_one, panel_two, precision=lax.Precision.HIGHEST)
    factor = jnp.linalg.cholesky(gram_matrix)
    leaf_basis = jax.scipy.linalg.solve_triangular(factor, jnp.swapaxes(panel_one, 1, 2), lower=True)
    reduced = jax.scipy.linalg.solve_triangular(factor, cross_gram, lower=True)
    leaf_miss = jnp.swapaxes(panel_two, 1, 2) - jnp.einsum('lst,lsa->lta', reduced, leaf_basis, precision=lax.Precision.HIGHEST)
    levels_local = LEAF_DEV.bit_length() - 1
    local_parts = []
    upper_basis = jnp.zeros((N_ROW, PANEL, 2 * PANEL), jnp.float32)
    current_factor, current_panel = (factor, reduced)
    for level_index in range(levels_local + LEVELS_UP):
        pair_count = current_factor.shape[0] // 2
        pair_factor = current_factor.reshape(pair_count, 2, PANEL, PANEL)
        pair_panel = current_panel.reshape(pair_count, 2, PANEL, PANEL)
        basis_level, current_factor, current_panel = combine(pair_factor[:, 0], pair_panel[:, 0], pair_factor[:, 1], pair_panel[:, 1])
        if level_index < levels_local:
            local_parts.append(basis_level.reshape(N_ROW, -1, PANEL, 2 * PANEL))
        else:
            rise = level_index - levels_local + 1
            target_rows = np.arange(pair_count, dtype=np.int32) * 2 ** rise + 2 ** (rise - 1)
            upper_basis = upper_basis.at[target_rows].set(basis_level)
    root_scale = 1.0 / math.sqrt(LEAVES * BLOCK)
    root_stack = jnp.concatenate([jnp.swapaxes(current_factor[0], 0, 1), current_panel[0]], axis=1) * root_scale
    upper_basis = upper_basis.at[0].set(root_stack)
    local_basis = jnp.concatenate(local_parts, axis=1).reshape(N_ROW * (LEAF_DEV - 1), PANEL, 2 * PANEL)
    return (leaf_basis, leaf_miss, local_basis, upper_basis)
```

```python
import math

import jax
import jax.numpy as jnp
from jax import lax
from jax.experimental import pallas as pl
from jax.experimental.pallas import tpu as pltpu
from jax.sharding import PartitionSpec as P

HIGHEST = lax.Precision.HIGHEST


def dot(left, right, dims):
    return lax.dot_general(
        left, right, (dims, ((), ())), precision=HIGHEST, preferred_element_type=jnp.float32
    )


def iota(shape, dim):
    return lax.broadcasted_iota(jnp.int32, shape, dim)


def factorize(m_ref, u_ref, group, block):
    n, width, _ = m_ref.shape
    sub = iota((n, 8, width), 1)
    lane = iota((n, 8, width), 2)

    def spread(value):
        return jnp.broadcast_to(value, (n, 8, width))

    for base in range(0, width, group):
        count = group // 8
        m = [m_ref[:, base + 8 * q : base + 8 * q + 8, :] for q in range(count)]
        for q in range(count):
            row = base + 8 * q
            diagonal = None
            upper = m[q]
            for start in range(0, 8, block):
                first = row + start
                e = {
                    i: [spread(m[i][:, :, first + k : first + k + 1]) for k in range(block)]
                    for i in range(q, count)
                }
                inside = (lane >= first) & (lane < first + block)
                for i in range(q, count):
                    fill = jnp.where((lane - row) == sub, 1.0, 0.0) if i == q else 0.0
                    m[i] = jnp.where(inside, fill, m[i])
                for k in range(block):
                    s = start + k
                    inverse = 1.0 / spread(e[q][k][:, s : s + 1, :])
                    pivot_row = spread(m[q][:, s : s + 1, :])
                    pivot_e = [spread(e[q][j][:, s : s + 1, :]) for j in range(k + 1, block)]
                    for i in range(q, count):
                        f = e[i][k] * inverse
                        if i == q:
                            f = jnp.where(sub > s, f, 0.0)
                        for j in range(k + 1, block):
                            e[i][j] = e[i][j] - f * pivot_e[j - k - 1]
                        m[i] = m[i] - f * pivot_row
                for k in range(block):
                    diagonal = e[q][k] if diagonal is None else jnp.where(sub >= start + k, e[q][k], diagonal)
                    upper = jnp.where(lane == first + k, e[q][k], upper)
            scale = lax.rsqrt(diagonal)
            inside = (lane >= row) & (lane < row + 8)
            u_ref[:, row : row + 8, :] = jnp.where(
                lane >= sub + row, jnp.where(inside, upper, m[q]) * scale, 0.0
            )
            m_ref[:, row : row + 8, :] = jnp.where(lane <= sub + row, m[q] * scale, 0.0)
        after = base + group
        if after < width:
            lane_rest = iota((width - after, width), 1)
            lane_panel = iota((group, width), 1)
            for b in range(n):
                u = u_ref[b, base:after, :]
                right = jnp.where(lane_panel < after, m_ref[b, base:after, :], u)
                update = dot(u, right, ((0,), (0,)))
                old = m_ref[b, after:, :]
                old = jnp.where((lane_rest >= base) & (lane_rest < after), 0.0, old)
                m_ref[b, after:, :] = old - update[after:]


def vmem():
    return pl.BlockSpec(memory_space=pltpu.VMEM)


def shape(*dims):
    return jax.ShapeDtypeStruct(dims, jnp.float32)


def near_products(offsets, near_blocks, low, own, high):
    leaf_count, _, size, _ = near_blocks.shape
    width = own.shape[2]

    def kernel(offset_ref, near_ref, low_ref, own_ref, high_ref, out_ref):
        offset = offset_ref[pl.program_id(0)]
        for part, ref in enumerate((low_ref, own_ref, high_ref)):

            @pl.when(offset // leaf_count == part)
            def _():
                out_ref[0] = dot(near_ref[0, 0], ref[0], ((1,), (0,)))

    def panel_spec(part):
        return pl.BlockSpec(
            (1, size, width),
            lambda i, offset_ref: (jnp.clip(offset_ref[i] - part * leaf_count, 0, leaf_count - 1), 0, 0),
        )

    return pl.pallas_call(
        kernel,
        grid_spec=pltpu.PrefetchScalarGridSpec(
            num_scalar_prefetch=1,
            grid=(leaf_count,),
            in_specs=[
                pl.BlockSpec((1, 1, size, size), lambda i, offset_ref: (i, 0, 0, 0)),
                panel_spec(0),
                panel_spec(1),
                panel_spec(2),
            ],
            out_specs=pl.BlockSpec((1, size, width), lambda i, offset_ref: (i, 0, 0)),
        ),
        out_shape=shape(leaf_count, size, width),
        name="near_products",
    )(offsets, near_blocks, low, own, high)


def leaf_grams(partial_sum, panel, nugget):
    size, width = panel.shape

    def kernel(sum_ref, panel_ref, nugget_ref, sample_ref, gram_ref):
        sample = sum_ref[...] + nugget_ref[...] * panel_ref[...]
        sample_ref[...] = sample
        gram_ref[...] = dot(sample[:, : width // 2], sample, ((0,), (0,)))

    return pl.pallas_call(
        kernel,
        in_specs=[vmem()] * 3,
        out_specs=[vmem()] * 2,
        out_shape=[shape(size, width), shape(width // 2, width)],
        name="leaf_grams",
    )(partial_sum, panel, nugget)


def node_children(leaf_count):
    level = [[i] for i in range(leaf_count)]
    nodes = []
    while len(level) > 1:
        pairs = [(level[2 * i], level[2 * i + 1]) for i in range(len(level) // 2)]
        nodes += pairs
        level = [a + b for a, b in pairs]
    return nodes


def local_sums(grams, row_count):
    leaf_count, rows, width = grams.shape
    half = width // 2
    nodes = node_children(leaf_count)
    nodes = nodes + [nodes[-1]] * (leaf_count - len(nodes))

    def kernel(grams_ref, local_ref, sums_ref):
        known = {(i,): grams_ref[i] for i in range(leaf_count)}
        for n, children in enumerate(nodes):
            a, b = tuple(children[0]), tuple(children[1])
            local_ref[n, 0] = known[a][:, :half]
            local_ref[n, 1] = known[b][:, :half]
            known[a + b] = known[a] + known[b]
        total = known[tuple(range(leaf_count))]
        sums_ref[...] = jnp.zeros_like(sums_ref)
        sums_ref[:rows] = total[:, :half]
        sums_ref[rows : 2 * rows] = total[:, half:]

    return pl.pallas_call(
        kernel,
        in_specs=[vmem()],
        out_specs=[vmem()] * 2,
        out_shape=[shape(leaf_count, 2, rows, half), shape(row_count, half)],
        name="local_sums",
    )(grams)


def tree_sums(rows_of_all):
    count, width = rows_of_all.shape

    def kernel(rows_ref, out_ref):
        r = iota((count, count), 0)
        s = iota((count, count), 1)
        stride = r & -r
        root = r == 0
        left = root | ((s >= r - stride) & (s < r))
        right = root | ((s >= r) & (s < r + stride))
        rows = rows_ref[...]
        out_ref[:, :width] = dot(jnp.where(left, 1.0, 0.0), rows, ((1,), (0,)))
        out_ref[:, width:] = dot(jnp.where(right, 1.0, 0.0), rows, ((1,), (0,)))

    return pl.pallas_call(
        kernel, in_specs=[vmem()], out_specs=vmem(), out_shape=shape(count, 2 * width), name="tree_sums"
    )(rows_of_all)


def gram_message(local, sums, row_index):
    leaf_count, _, rows, half = local.shape

    def kernel(row_ref, local_ref, sums_ref, out_ref):
        root = row_ref[0] == 0
        a = sums_ref[:rows, :half]
        b = sums_ref[:rows, half:]
        cross = sums_ref[rows : 2 * rows, :half]
        total = jnp.where(root, a, a + b)
        for c in range(leaf_count):
            out_ref[c, 0] = local_ref[c, 0]
            out_ref[c, 1] = local_ref[c, 1]
            out_ref[c, 2] = jnp.where(root, cross, a if c < leaf_count // 2 else b)
            out_ref[c, 3] = total

    return pl.pallas_call(
        kernel,
        in_specs=[pl.BlockSpec(memory_space=pltpu.SMEM), vmem(), vmem()],
        out_specs=vmem(),
        out_shape=shape(leaf_count, 4, rows, half),
        name="gram_message",
    )(row_index, local, sums)


def node_bases(index, received, gram, sample, root_scale):
    parts, _, rows, half = received.shape
    size, width = sample.shape
    share = width // parts

    def kernel(index_ref, received_ref, gram_ref, sample_ref, message_ref, upper_ref, m_ref, u_ref):
        for c in range(parts):
            piece = slice(rows * c, rows * (c + 1))
            a, b = received_ref[c, 0], received_ref[c, 1]
            m_ref[0, piece, :] = gram_ref[piece, :half]
            m_ref[1, piece, :] = a
            m_ref[2, piece, :] = b
            m_ref[3, piece, :] = a + b
            m_ref[4, piece, :] = received_ref[c, 2]
            m_ref[5, piece, :] = received_ref[c, 3]
        factorize(m_ref, u_ref, 32, 8)
        inverse = m_ref[0]
        basis = dot(sample_ref[:, :half], inverse, ((1,), (1,)))
        reduced = dot(inverse, gram_ref[:, half:], ((1,), (0,)))
        missed = sample_ref[:, half:] - dot(basis, reduced, ((1,), (0,)))
        node_a = dot(u_ref[1], m_ref[3], ((1,), (1,)))
        node_b = dot(u_ref[2], m_ref[3], ((1,), (1,)))
        for c in range(parts):
            message_ref[c, 0] = basis[share * c : share * (c + 1)]
            message_ref[c, 1] = missed[share * c : share * (c + 1)]
            node = node_a if c < parts // 2 else node_b
            at = share * (c % (parts // 2))
            message_ref[c, 2] = node[at : at + share]
        root = index_ref[0] == 0
        column = index_ref[1]

        @pl.when(root)
        def _():
            for c in range(parts):
                piece = slice(rows * c, rows * (c + 1))
                u_ref[4, piece, :] = received_ref[c, 2]

        at = pl.multiple_of(share * lax.rem(column, parts // 2), share)

        @pl.when(jnp.logical_not(root))
        def _():
            upper_ref[...] = dot(m_ref[5], u_ref[4, pl.ds(at, share), :], ((1,), (1,)))

        @pl.when(root)
        def _():
            reduced_root = dot(m_ref[5], u_ref[4], ((1,), (0,)))
            u_ref[0] = jnp.where(column < parts // 2, u_ref[5], reduced_root).T * root_scale
            upper_ref[...] = u_ref[0, pl.ds(at, share), :].T

    return pl.pallas_call(
        kernel,
        in_specs=[pl.BlockSpec(memory_space=pltpu.SMEM), vmem(), vmem(), vmem()],
        out_specs=[vmem()] * 2,
        out_shape=[shape(parts, 3, share, half), shape(half, share)],
        scratch_shapes=[pltpu.VMEM((6, half, half), jnp.float32)] * 2,
        name="node_bases",
    )(index, received, gram, sample)


def placed_outputs(received):
    parts, _, share, half = received.shape

    def kernel(received_ref, basis_ref, miss_ref, local_ref):
        for c in range(parts):
            basis_ref[c] = received_ref[c, 0].T
            miss_ref[c] = received_ref[c, 1].T
            if c < parts - 1:
                local_ref[c] = received_ref[c, 2].T

    return pl.pallas_call(
        kernel,
        in_specs=[vmem()],
        out_specs=[vmem()] * 3,
        out_shape=[shape(parts, half, share), shape(parts, half, share), shape(parts - 1, half, share)],
        name="placed_outputs",
    )(received)


def neighbours(block):
    count = lax.axis_size("row")
    forward = [(i, i + 1) for i in range(count - 1)]
    backward = [(i + 1, i) for i in range(count - 1)]
    return lax.ppermute(block, "row", forward), lax.ppermute(block, "row", backward)


def exchange(block, axis):
    return lax.all_to_all(block, axis, 0, 0, tiled=True)


def on_device(near_blocks, column_block, test_panels, nugget):
    leaf_count = near_blocks.shape[0]
    size = near_blocks.shape[2]
    half = test_panels.shape[2] // 2
    row_count = lax.axis_size("row")
    col_count = lax.axis_size("col")
    row_index = lax.axis_index("row")
    col_index = lax.axis_index("col")
    index = jnp.stack([row_index, col_index]).astype(jnp.int32)
    offsets = (column_block - (row_index - 1) * leaf_count).reshape(-1)

    own = lax.all_gather(test_panels, "col", axis=0, tiled=True)
    low, high = neighbours(own)
    partial_sums = near_products(offsets, near_blocks, low, own, high)
    summed = lax.psum_scatter(partial_sums, "col", scatter_dimension=0, tiled=True)
    own_nugget = lax.dynamic_slice_in_dim(nugget, col_index, 1, 0).reshape(size, 1)
    sample, gram = leaf_grams(summed[0], test_panels[0], own_nugget)

    grams = exchange(gram.reshape(col_count, half // col_count, 2 * half), "col")
    local, sums = local_sums(grams, row_count)
    sums = exchange(tree_sums(exchange(sums, "row")), "row")
    received = exchange(gram_message(local, sums, index), "col")
    root_scale = 1.0 / math.sqrt(leaf_count * row_count * size)
    message, upper = node_bases(index, received, gram, sample, root_scale)
    leaf_basis, leaf_miss, local_basis = placed_outputs(exchange(message, "col"))
    return leaf_basis, leaf_miss, local_basis, upper[None]


def solution(mesh):
    placed = (
        P("row", "col", None, None),
        P("row", "col"),
        P(("row", "col"), None, None),
        P("row", None),
    )
    return jax.shard_map(
        on_device,
        mesh=mesh,
        in_specs=placed,
        out_specs=(P("row", None, "col"),) * 4,
        check_vma=False,
    )
```

```python
import math

import jax
import jax.numpy as jnp
from jax import lax
from jax.experimental import pallas as pl
from jax.experimental.pallas import tpu as pltpu
from jax.sharding import PartitionSpec as P

HIGHEST = lax.Precision.HIGHEST


def dot(left, right, dims):
    return lax.dot_general(
        left, right, (dims, ((), ())), precision=HIGHEST, preferred_element_type=jnp.float32
    )


def iota(shape, dim):
    return lax.broadcasted_iota(jnp.int32, shape, dim)


def factorize(m_ref, u_ref, group, block):
    n, width, _ = m_ref.shape
    sub = iota((n, 8, width), 1)
    lane = iota((n, 8, width), 2)

    def spread(value):
        return jnp.broadcast_to(value, (n, 8, width))

    for base in range(0, width, group):
        count = group // 8
        m = [m_ref[:, base + 8 * q : base + 8 * q + 8, :] for q in range(count)]
        for q in range(count):
            row = base + 8 * q
            diagonal = None
            upper = m[q]
            for start in range(0, 8, block):
                first = row + start
                e = {
                    i: [spread(m[i][:, :, first + k : first + k + 1]) for k in range(block)]
                    for i in range(q, count)
                }
                inside = (lane >= first) & (lane < first + block)
                for i in range(q, count):
                    fill = jnp.where((lane - row) == sub, 1.0, 0.0) if i == q else 0.0
                    m[i] = jnp.where(inside, fill, m[i])
                for k in range(block):
                    s = start + k
                    inverse = 1.0 / spread(e[q][k][:, s : s + 1, :])
                    pivot_row = spread(m[q][:, s : s + 1, :])
                    pivot_e = [spread(e[q][j][:, s : s + 1, :]) for j in range(k + 1, block)]
                    for i in range(q, count):
                        f = e[i][k] * inverse
                        if i == q:
                            f = jnp.where(sub > s, f, 0.0)
                        for j in range(k + 1, block):
                            e[i][j] = e[i][j] - f * pivot_e[j - k - 1]
                        m[i] = m[i] - f * pivot_row
                for k in range(block):
                    diagonal = e[q][k] if diagonal is None else jnp.where(sub >= start + k, e[q][k], diagonal)
                    upper = jnp.where(lane == first + k, e[q][k], upper)
            scale = lax.rsqrt(diagonal)
            inside = (lane >= row) & (lane < row + 8)
            u_ref[:, row : row + 8, :] = jnp.where(
                lane >= sub + row, jnp.where(inside, upper, m[q]) * scale, 0.0
            )
            m_ref[:, row : row + 8, :] = jnp.where(lane <= sub + row, m[q] * scale, 0.0)
        after = base + group
        if after < width:
            lane_rest = iota((width - after, width), 1)
            lane_panel = iota((group, width), 1)
            for b in range(n):
                u = u_ref[b, base:after, :]
                right = jnp.where(lane_panel < after, m_ref[b, base:after, :], u)
                update = dot(u, right, ((0,), (0,)))
                old = m_ref[b, after:, :]
                old = jnp.where((lane_rest >= base) & (lane_rest < after), 0.0, old)
                m_ref[b, after:, :] = old - update[after:]


def vmem():
    return pl.BlockSpec(memory_space=pltpu.VMEM)


def shape(*dims):
    return jax.ShapeDtypeStruct(dims, jnp.float32)


def near_products(index, offsets, near_blocks, own, low, high, targets):
    parts, _, size, _ = near_blocks.shape
    width = own[0].shape[-1]
    count = len(targets)
    groups = [low, own, high]
    operands = [piece for group in groups for piece in group]

    def kernel(index_ref, offset_ref, near_ref, *refs):
        panels, (out_ref, near_buffer, panel_buffer, sems) = refs[: len(operands)], refs[len(operands) :]
        column = index_ref[1]
        for i, target in enumerate(targets):
            leaf = lax.rem(column + target, parts)
            offset = offset_ref[leaf]
            row_part = offset // parts
            back = lax.rem(column - lax.rem(offset, parts) + parts + AHEAD, parts)
            pltpu.make_async_copy(near_ref.at[leaf, 0], near_buffer.at[i], sems.at[0, i]).start()
            at = 0
            for g, group in enumerate(groups):
                first = 0
                for piece in group:
                    length = piece.shape[0]
                    ref, begin = panels[at], first

                    @pl.when((row_part == g) & (back >= begin) & (back < begin + length))
                    def _():
                        pltpu.make_async_copy(
                            ref.at[back - begin if length > 1 else 0], panel_buffer.at[i], sems.at[1, i]
                        ).start()

                    at += 1
                    first += length
        for i in range(count):
            pltpu.make_async_copy(near_ref.at[0, 0], near_buffer.at[i], sems.at[0, i]).wait()
            pltpu.make_async_copy(panels[0].at[0], panel_buffer.at[i], sems.at[1, i]).wait()
            out_ref[i] = dot(near_buffer[i], panel_buffer[i], ((1,), (0,)))

    anywhere = pl.BlockSpec(memory_space=pl.ANY)
    smem = pl.BlockSpec(memory_space=pltpu.SMEM)
    return pl.pallas_call(
        kernel,
        in_specs=[smem, smem, anywhere] + [anywhere] * len(operands),
        out_specs=vmem(),
        out_shape=shape(count, size, width),
        scratch_shapes=[
            pltpu.VMEM((count, size, size), jnp.float32),
            pltpu.VMEM((count, size, width), jnp.float32),
            pltpu.SemaphoreType.DMA((2, count)),
        ],
        cost_estimate=pl.CostEstimate(
            flops=12 * count * size * size * width,
            bytes_accessed=12 * count * size * width,
            transcendentals=0,
        ),
        name="near_products",
    )(index, offsets, near_blocks, *operands)


def leaf_grams(index, left, right, products, panel, nugget):
    _, size, width = panel.shape

    def kernel(index_ref, left_ref, right_ref, product_ref, panel_ref, nugget_ref, sample_ref, gram_ref):
        row = nugget_ref[pl.ds(index_ref[1], 1), :]
        column = jnp.broadcast_to(row, (8, size)).T[:, :1]
        sample = left_ref[0] + right_ref[0] + product_ref[0] + column * panel_ref[0]
        sample_ref[...] = sample
        gram_ref[...] = dot(sample[:, : width // 2], sample, ((0,), (0,)))

    return pl.pallas_call(
        kernel,
        grid=(1,),
        in_specs=[
            pl.BlockSpec(memory_space=pltpu.SMEM),
            vmem(),
            vmem(),
            pl.BlockSpec((1, size, width), lambda i: (products.shape[0] - 1, 0, 0)),
            vmem(),
            vmem(),
        ],
        out_specs=[vmem()] * 2,
        out_shape=[shape(size, width), shape(width // 2, width)],
        name="leaf_grams",
    )(index, left, right, products, panel, nugget)


def node_children(leaf_count):
    level = [[i] for i in range(leaf_count)]
    nodes = []
    while len(level) > 1:
        pairs = [(level[2 * i], level[2 * i + 1]) for i in range(len(level) // 2)]
        nodes += pairs
        level = [a + b for a, b in pairs]
    return nodes


def local_sums(grams, row_count):
    leaf_count, rows, width = grams.shape
    half = width // 2
    nodes = node_children(leaf_count)
    nodes = nodes + [nodes[-1]] * (leaf_count - len(nodes))

    def kernel(grams_ref, local_ref, sums_ref):
        known = {(i,): grams_ref[i] for i in range(leaf_count)}
        for n, children in enumerate(nodes):
            a, b = tuple(children[0]), tuple(children[1])
            local_ref[n, 0] = known[a][:, :half]
            local_ref[n, 1] = known[b][:, :half]
            known[a + b] = known[a] + known[b]
        total = known[tuple(range(leaf_count))]
        sums_ref[...] = jnp.zeros_like(sums_ref)
        sums_ref[:rows] = total[:, :half]
        sums_ref[rows : 2 * rows] = total[:, half:]

    return pl.pallas_call(
        kernel,
        in_specs=[vmem()],
        out_specs=[vmem()] * 2,
        out_shape=[shape(leaf_count, 2, rows, half), shape(row_count, half)],
        name="local_sums",
    )(grams)


def tree_sums(rows_of_all):
    count, width = rows_of_all.shape

    def kernel(rows_ref, out_ref):
        r = iota((count, count), 0)
        s = iota((count, count), 1)
        stride = r & -r
        root = r == 0
        left = root | ((s >= r - stride) & (s < r))
        right = root | ((s >= r) & (s < r + stride))
        rows = rows_ref[...]
        out_ref[:, :width] = dot(jnp.where(left, 1.0, 0.0), rows, ((1,), (0,)))
        out_ref[:, width:] = dot(jnp.where(right, 1.0, 0.0), rows, ((1,), (0,)))

    return pl.pallas_call(
        kernel, in_specs=[vmem()], out_specs=vmem(), out_shape=shape(count, 2 * width), name="tree_sums"
    )(rows_of_all)


def gram_message(local, sums, row_index):
    leaf_count, _, rows, half = local.shape

    def kernel(row_ref, local_ref, sums_ref, out_ref):
        root = row_ref[0] == 0
        a = sums_ref[:rows, :half]
        b = sums_ref[:rows, half:]
        cross = sums_ref[rows : 2 * rows, :half]
        total = jnp.where(root, a, a + b)
        for c in range(leaf_count):
            out_ref[c, 0] = local_ref[c, 0]
            out_ref[c, 1] = local_ref[c, 1]
            out_ref[c, 2] = jnp.where(root, cross, a if c < leaf_count // 2 else b)
            out_ref[c, 3] = total

    return pl.pallas_call(
        kernel,
        in_specs=[pl.BlockSpec(memory_space=pltpu.SMEM), vmem(), vmem()],
        out_specs=vmem(),
        out_shape=shape(leaf_count, 4, rows, half),
        name="gram_message",
    )(row_index, local, sums)


def node_bases(index, received, gram, sample, root_scale):
    parts, _, rows, half = received.shape
    size, width = sample.shape
    share = width // parts

    def kernel(index_ref, received_ref, gram_ref, sample_ref, message_ref, upper_ref, m_ref, u_ref):
        for c in range(parts):
            piece = slice(rows * c, rows * (c + 1))
            a, b = received_ref[c, 0], received_ref[c, 1]
            m_ref[0, piece, :] = gram_ref[piece, :half]
            m_ref[1, piece, :] = a
            m_ref[2, piece, :] = b
            m_ref[3, piece, :] = a + b
            m_ref[4, piece, :] = received_ref[c, 2]
            m_ref[5, piece, :] = received_ref[c, 3]
        factorize(m_ref, u_ref, 32, 8)
        inverse = m_ref[0]
        basis = dot(sample_ref[:, :half], inverse, ((1,), (1,)))
        reduced = dot(inverse, gram_ref[:, half:], ((1,), (0,)))
        missed = sample_ref[:, half:] - dot(basis, reduced, ((1,), (0,)))
        node_a = dot(u_ref[1], m_ref[3], ((1,), (1,)))
        node_b = dot(u_ref[2], m_ref[3], ((1,), (1,)))
        for c in range(parts):
            message_ref[c, 0] = basis[share * c : share * (c + 1)]
            message_ref[c, 1] = missed[share * c : share * (c + 1)]
            node = node_a if c < parts // 2 else node_b
            at = share * (c % (parts // 2))
            message_ref[c, 2] = node[at : at + share]
        root = index_ref[0] == 0
        column = index_ref[1]

        @pl.when(root)
        def _():
            for c in range(parts):
                piece = slice(rows * c, rows * (c + 1))
                u_ref[4, piece, :] = received_ref[c, 2]

        at = pl.multiple_of(share * lax.rem(column, parts // 2), share)

        @pl.when(jnp.logical_not(root))
        def _():
            upper_ref[...] = dot(u_ref[4, pl.ds(at, share), :], m_ref[5], ((1,), (1,)))

        @pl.when(root)
        def _():
            reduced_root = dot(m_ref[5], u_ref[4], ((1,), (0,)))
            u_ref[0] = jnp.where(column < parts // 2, u_ref[5], reduced_root).T * root_scale
            upper_ref[...] = u_ref[0, pl.ds(at, share), :]

    return pl.pallas_call(
        kernel,
        in_specs=[pl.BlockSpec(memory_space=pltpu.SMEM), vmem(), vmem(), vmem()],
        out_specs=[vmem()] * 2,
        out_shape=[shape(parts, 3, share, half), shape(share, half)],
        scratch_shapes=[pltpu.VMEM((6, half, half), jnp.float32)] * 2,
        name="node_bases",
    )(index, received, gram, sample)


def neighbours(block):
    count = lax.axis_size("row")
    forward = [(i, i + 1) for i in range(count - 1)]
    backward = [(i + 1, i) for i in range(count - 1)]
    return lax.ppermute(block, "row", forward), lax.ppermute(block, "row", backward)


def along_col(block, step):
    count = lax.axis_size("col")
    return lax.ppermute(block, "col", [(i, (i + step) % count) for i in range(count)])


def gathered(block):
    back, ahead = [block], [block]
    for _ in range(2):
        back.append(along_col(back[-1], 1))
        ahead.append(along_col(ahead[-1], -1))
    first = [ahead[2], ahead[1], block, back[1], back[2]]
    low_first, high_first = neighbours(jnp.concatenate(first, axis=0))
    three_back = along_col(back[2], 1)
    three_ahead = along_col(ahead[2], -1)
    second = [three_back, along_col(three_back, 1), three_ahead]
    low_second, high_second = neighbours(jnp.concatenate(second, axis=0))
    return first + second, [low_first, low_second], [high_first, high_second]


AHEAD = 2


def exchange(block, axis):
    return lax.all_to_all(block, axis, 0, 0, tiled=True)


def on_device(near_blocks, column_block, test_panels, nugget):
    leaf_count = near_blocks.shape[0]
    size = near_blocks.shape[2]
    half = test_panels.shape[2] // 2
    row_count = lax.axis_size("row")
    col_count = lax.axis_size("col")
    row_index = lax.axis_index("row")
    col_index = lax.axis_index("col")
    index = jnp.stack([row_index, col_index]).astype(jnp.int32)
    offsets = (column_block - (row_index - 1) * leaf_count).reshape(-1)

    own, low, high = gathered(test_panels)
    far = near_products(index, offsets, near_blocks, own, low, high, (4, 3))
    rest = near_products(index, offsets, near_blocks, own, low, high, (5, 2, 6, 1, 7, 0))
    right = along_col(far[:1], -1)
    left = along_col(far[1:], 1)
    right = along_col(right + rest[0:1], -1)
    left = along_col(left + rest[1:2], 1)
    right = along_col(right + rest[2:3], -1)
    left = along_col(left + rest[3:4], 1)
    right = along_col(right + rest[4:5], -1)
    sample, gram = leaf_grams(index, left, right, rest, test_panels, nugget)

    grams = exchange(gram.reshape(col_count, half // col_count, 2 * half), "col")
    local, sums = local_sums(grams, row_count)
    sums = exchange(tree_sums(exchange(sums, "row")), "row")
    received = exchange(gram_message(local, sums, index), "col")
    root_scale = 1.0 / math.sqrt(leaf_count * row_count * size)
    message, upper = node_bases(index, received, gram, sample, root_scale)
    outputs = exchange(message, "col")
    stored = (outputs[:, 0], outputs[:, 1], outputs[: col_count - 1, 2], upper[None])
    return tuple(jnp.swapaxes(output, 1, 2) for output in stored)


def solution(mesh):
    placed = (
        P("row", "col", None, None),
        P("row", "col"),
        P(("row", "col"), None, None),
        P("row", None),
    )
    return jax.shard_map(
        on_device,
        mesh=mesh,
        in_specs=placed,
        out_specs=(P("row", None, "col"),) * 4,
        check_vma=False,
    )
```

```python
import math

import jax
import jax.numpy as jnp
from jax import lax
from jax.experimental import pallas as pl
from jax.experimental.pallas import tpu as pltpu
from jax.sharding import PartitionSpec as P

HIGHEST = lax.Precision.HIGHEST


def dot(left, right, dims):
    return lax.dot_general(
        left, right, (dims, ((), ())), precision=HIGHEST, preferred_element_type=jnp.float32
    )


def iota(shape, dim):
    return lax.broadcasted_iota(jnp.int32, shape, dim)


def factorize(m_ref, u_ref, group, block):
    n, width, _ = m_ref.shape
    sub = iota((n, 8, width), 1)
    lane = iota((n, 8, width), 2)

    def spread(value):
        return jnp.broadcast_to(value, (n, 8, width))

    for base in range(0, width, group):
        count = group // 8
        m = [m_ref[:, base + 8 * q : base + 8 * q + 8, :] for q in range(count)]
        for q in range(count):
            row = base + 8 * q
            diagonal = None
            upper = m[q]
            for start in range(0, 8, block):
                first = row + start
                e = {
                    i: [spread(m[i][:, :, first + k : first + k + 1]) for k in range(block)]
                    for i in range(q, count)
                }
                inside = (lane >= first) & (lane < first + block)
                for i in range(q, count):
                    fill = jnp.where((lane - row) == sub, 1.0, 0.0) if i == q else 0.0
                    m[i] = jnp.where(inside, fill, m[i])
                for k in range(block):
                    s = start + k
                    inverse = 1.0 / spread(e[q][k][:, s : s + 1, :])
                    pivot_row = spread(m[q][:, s : s + 1, :])
                    pivot_e = [spread(e[q][j][:, s : s + 1, :]) for j in range(k + 1, block)]
                    for i in range(q, count):
                        f = e[i][k] * inverse
                        if i == q:
                            f = jnp.where(sub > s, f, 0.0)
                        for j in range(k + 1, block):
                            e[i][j] = e[i][j] - f * pivot_e[j - k - 1]
                        m[i] = m[i] - f * pivot_row
                for k in range(block):
                    diagonal = e[q][k] if diagonal is None else jnp.where(sub >= start + k, e[q][k], diagonal)
                    upper = jnp.where(lane == first + k, e[q][k], upper)
            scale = lax.rsqrt(diagonal)
            inside = (lane >= row) & (lane < row + 8)
            u_ref[:, row : row + 8, :] = jnp.where(
                lane >= sub + row, jnp.where(inside, upper, m[q]) * scale, 0.0
            )
            m_ref[:, row : row + 8, :] = jnp.where(lane <= sub + row, m[q] * scale, 0.0)
        after = base + group
        if after < width:
            lane_rest = iota((width - after, width), 1)
            lane_panel = iota((group, width), 1)
            for b in range(n):
                u = u_ref[b, base:after, :]
                right = jnp.where(lane_panel < after, m_ref[b, base:after, :], u)
                update = dot(u, right, ((0,), (0,)))
                old = m_ref[b, after:, :]
                old = jnp.where((lane_rest >= base) & (lane_rest < after), 0.0, old)
                m_ref[b, after:, :] = old - update[after:]


def vmem():
    return pl.BlockSpec(memory_space=pltpu.VMEM)


def shape(*dims):
    return jax.ShapeDtypeStruct(dims, jnp.float32)


def leaf_sample(index, offsets, near, panels, panel, nugget):
    parts, size, width = panels[0].shape
    split = size // 2

    def kernel(index_ref, offset_ref, near_ref, more_ref, *refs):
        panel_refs, (panel_ref, nugget_ref, sample_ref, gram_ref, buffer, sems) = refs[:3], refs[3:]
        for k in range(parts):
            offset = offset_ref[k]
            for part, ref in enumerate(panel_refs):

                @pl.when(offset // parts == part)
                def _():
                    pltpu.make_async_copy(ref.at[lax.rem(offset, parts)], buffer.at[k], sems.at[k]).start()

        row = nugget_ref[pl.ds(index_ref[1], 1), :]
        column = jnp.broadcast_to(row, (8, size)).T[:, :1]
        sample_ref[...] = column * panel_ref[0]
        for k in range(parts):
            pltpu.make_async_copy(panel_refs[0].at[0], buffer.at[k], sems.at[k]).wait()
            sample_ref[:split] += dot(near_ref[k, :split], buffer[k], ((1,), (0,)))
            sample_ref[split:] += dot(more_ref[k], buffer[k], ((1,), (0,)))
        gram_ref[...] = dot(sample_ref[:, : width // 2], sample_ref[...], ((0,), (0,)))

    anywhere = pl.BlockSpec(memory_space=pl.ANY)
    smem = pl.BlockSpec(memory_space=pltpu.SMEM)
    return pl.pallas_call(
        kernel,
        in_specs=[smem, smem, vmem(), vmem()] + [anywhere] * 3 + [vmem()] * 2,
        out_specs=[vmem()] * 2,
        out_shape=[shape(size, width), shape(width // 2, width)],
        scratch_shapes=[pltpu.VMEM((parts, size, width), jnp.float32), pltpu.SemaphoreType.DMA((parts,))],
        name="leaf_sample",
    )(index, offsets, *near, *panels, panel, nugget)


def node_children(leaf_count):
    level = [[i] for i in range(leaf_count)]
    nodes = []
    while len(level) > 1:
        pairs = [(level[2 * i], level[2 * i + 1]) for i in range(len(level) // 2)]
        nodes += pairs
        level = [a + b for a, b in pairs]
    return nodes


def local_sums(grams, row_count):
    leaf_count, rows, width = grams.shape
    half = width // 2
    nodes = node_children(leaf_count)
    nodes = nodes + [nodes[-1]] * (leaf_count - len(nodes))

    def kernel(grams_ref, local_ref, sums_ref):
        known = {(i,): grams_ref[i] for i in range(leaf_count)}
        for n, children in enumerate(nodes):
            a, b = tuple(children[0]), tuple(children[1])
            local_ref[n, 0] = known[a][:, :half]
            local_ref[n, 1] = known[b][:, :half]
            known[a + b] = known[a] + known[b]
        total = known[tuple(range(leaf_count))]
        sums_ref[...] = jnp.zeros_like(sums_ref)
        sums_ref[:rows] = total[:, :half]
        sums_ref[rows : 2 * rows] = total[:, half:]

    return pl.pallas_call(
        kernel,
        in_specs=[vmem()],
        out_specs=[vmem()] * 2,
        out_shape=[shape(leaf_count, 2, rows, half), shape(row_count, half)],
        name="local_sums",
    )(grams)


def tree_sums(rows_of_all):
    count, width = rows_of_all.shape

    def kernel(rows_ref, out_ref):
        r = iota((count, count), 0)
        s = iota((count, count), 1)
        stride = r & -r
        root = r == 0
        left = root | ((s >= r - stride) & (s < r))
        right = root | ((s >= r) & (s < r + stride))
        rows = rows_ref[...]
        out_ref[:, :width] = dot(jnp.where(left, 1.0, 0.0), rows, ((1,), (0,)))
        out_ref[:, width:] = dot(jnp.where(right, 1.0, 0.0), rows, ((1,), (0,)))

    return pl.pallas_call(
        kernel, in_specs=[vmem()], out_specs=vmem(), out_shape=shape(count, 2 * width), name="tree_sums"
    )(rows_of_all)


def gram_message(local, sums, row_index):
    leaf_count, _, rows, half = local.shape

    def kernel(row_ref, local_ref, sums_ref, out_ref):
        root = row_ref[0] == 0
        a = sums_ref[:rows, :half]
        b = sums_ref[:rows, half:]
        cross = sums_ref[rows : 2 * rows, :half]
        total = jnp.where(root, a, a + b)
        for c in range(leaf_count):
            out_ref[c, 0] = local_ref[c, 0]
            out_ref[c, 1] = local_ref[c, 1]
            out_ref[c, 2] = jnp.where(root, cross, a if c < leaf_count // 2 else b)
            out_ref[c, 3] = total

    return pl.pallas_call(
        kernel,
        in_specs=[pl.BlockSpec(memory_space=pltpu.SMEM), vmem(), vmem()],
        out_specs=vmem(),
        out_shape=shape(leaf_count, 4, rows, half),
        name="gram_message",
    )(row_index, local, sums)


def node_bases(index, received, gram, sample, root_scale):
    parts, _, rows, half = received.shape
    size, width = sample.shape
    share = width // parts

    def kernel(index_ref, received_ref, gram_ref, sample_ref, message_ref, upper_ref, m_ref, u_ref):
        for c in range(parts):
            piece = slice(rows * c, rows * (c + 1))
            a, b = received_ref[c, 0], received_ref[c, 1]
            m_ref[0, piece, :] = gram_ref[piece, :half]
            m_ref[1, piece, :] = a
            m_ref[2, piece, :] = b
            m_ref[3, piece, :] = a + b
            m_ref[4, piece, :] = received_ref[c, 2]
            m_ref[5, piece, :] = received_ref[c, 3]
        factorize(m_ref, u_ref, 32, 8)
        inverse = m_ref[0]
        basis = dot(sample_ref[:, :half], inverse, ((1,), (1,)))
        reduced = dot(inverse, gram_ref[:, half:], ((1,), (0,)))
        missed = sample_ref[:, half:] - dot(basis, reduced, ((1,), (0,)))
        node_a = dot(u_ref[1], m_ref[3], ((1,), (1,)))
        node_b = dot(u_ref[2], m_ref[3], ((1,), (1,)))
        for c in range(parts):
            message_ref[c, 0] = basis[share * c : share * (c + 1)]
            message_ref[c, 1] = missed[share * c : share * (c + 1)]
            node = node_a if c < parts // 2 else node_b
            at = share * (c % (parts // 2))
            message_ref[c, 2] = node[at : at + share]
        root = index_ref[0] == 0
        column = index_ref[1]

        @pl.when(root)
        def _():
            for c in range(parts):
                piece = slice(rows * c, rows * (c + 1))
                u_ref[4, piece, :] = received_ref[c, 2]

        at = pl.multiple_of(share * lax.rem(column, parts // 2), share)

        @pl.when(jnp.logical_not(root))
        def _():
            upper_ref[...] = dot(u_ref[4, pl.ds(at, share), :], m_ref[5], ((1,), (1,)))

        @pl.when(root)
        def _():
            reduced_root = dot(m_ref[5], u_ref[4], ((1,), (0,)))
            u_ref[0] = jnp.where(column < parts // 2, u_ref[5], reduced_root).T * root_scale
            upper_ref[...] = u_ref[0, pl.ds(at, share), :]

    return pl.pallas_call(
        kernel,
        in_specs=[pl.BlockSpec(memory_space=pltpu.SMEM), vmem(), vmem(), vmem()],
        out_specs=[vmem()] * 2,
        out_shape=[shape(parts, 3, share, half), shape(share, half)],
        scratch_shapes=[pltpu.VMEM((6, half, half), jnp.float32)] * 2,
        name="node_bases",
    )(index, received, gram, sample)


def neighbours(block):
    count = lax.axis_size("row")
    forward = [(i, i + 1) for i in range(count - 1)]
    backward = [(i + 1, i) for i in range(count - 1)]
    return lax.ppermute(block, "row", forward), lax.ppermute(block, "row", backward)


def exchange(block, axis):
    return lax.all_to_all(block, axis, 0, 0, tiled=True)


def on_device(near_blocks, column_block, test_panels, nugget):
    leaf_count = near_blocks.shape[0]
    size = near_blocks.shape[2]
    half = test_panels.shape[2] // 2
    row_count = lax.axis_size("row")
    col_count = lax.axis_size("col")
    row_index = lax.axis_index("row")
    col_index = lax.axis_index("col")
    index = jnp.stack([row_index, col_index]).astype(jnp.int32)

    split = size // 2
    number = jnp.broadcast_to(column_block[:, :, None].astype(jnp.float32), (leaf_count, 8, size))
    near = exchange(jnp.concatenate([near_blocks[:, 0, :split], number], axis=1), "col")
    own = lax.all_gather(test_panels, "col", axis=0, tiled=True)
    rest, own = lax.optimization_barrier((near_blocks[:, 0, split:], own))
    low, high = neighbours(own)
    more = exchange(rest, "col")
    offsets = near[:, split, 0].astype(jnp.int32) - (row_index - 1) * leaf_count
    sample, gram = leaf_sample(index, offsets, (near, more), (low, own, high), test_panels, nugget)

    grams = exchange(gram.reshape(col_count, half // col_count, 2 * half), "col")
    local, sums = local_sums(grams, row_count)
    sums = exchange(tree_sums(exchange(sums, "row")), "row")
    received = exchange(gram_message(local, sums, index), "col")
    root_scale = 1.0 / math.sqrt(leaf_count * row_count * size)
    message, upper = node_bases(index, received, gram, sample, root_scale)
    outputs = exchange(message, "col")
    stored = (outputs[:, 0], outputs[:, 1], outputs[: col_count - 1, 2], upper[None])
    return tuple(jnp.swapaxes(output, 1, 2) for output in stored)


def solution(mesh):
    placed = (
        P("row", "col", None, None),
        P("row", "col"),
        P(("row", "col"), None, None),
        P("row", None),
    )
    return jax.shard_map(
        on_device,
        mesh=mesh,
        in_specs=placed,
        out_specs=(P("row", None, "col"),) * 4,
        check_vma=False,
    )
```

```python
import math

import jax
import jax.numpy as jnp
from jax import lax
from jax.experimental import pallas as pl
from jax.experimental.pallas import tpu as pltpu
from jax.sharding import PartitionSpec as P

HIGHEST = lax.Precision.HIGHEST


def dot(left, right, dims):
    return lax.dot_general(
        left, right, (dims, ((), ())), precision=HIGHEST, preferred_element_type=jnp.float32
    )


def iota(shape, dim):
    return lax.broadcasted_iota(jnp.int32, shape, dim)


def factorize(m_ref, u_ref, group, block):
    n, width, _ = m_ref.shape
    sub = iota((n, 8, width), 1)
    lane = iota((n, 8, width), 2)

    def spread(value):
        return jnp.broadcast_to(value, (n, 8, width))

    for base in range(0, width, group):
        count = group // 8
        m = [m_ref[:, base + 8 * q : base + 8 * q + 8, :] for q in range(count)]
        for q in range(count):
            row = base + 8 * q
            diagonal = None
            upper = m[q]
            for start in range(0, 8, block):
                first = row + start
                e = {
                    i: [spread(m[i][:, :, first + k : first + k + 1]) for k in range(block)]
                    for i in range(q, count)
                }
                inside = (lane >= first) & (lane < first + block)
                for i in range(q, count):
                    fill = jnp.where((lane - row) == sub, 1.0, 0.0) if i == q else 0.0
                    m[i] = jnp.where(inside, fill, m[i])
                for k in range(block):
                    s = start + k
                    inverse = 1.0 / spread(e[q][k][:, s : s + 1, :])
                    pivot_row = spread(m[q][:, s : s + 1, :])
                    pivot_e = [spread(e[q][j][:, s : s + 1, :]) for j in range(k + 1, block)]
                    for i in range(q, count):
                        f = e[i][k] * inverse
                        if i == q:
                            f = jnp.where(sub > s, f, 0.0)
                        for j in range(k + 1, block):
                            e[i][j] = e[i][j] - f * pivot_e[j - k - 1]
                        m[i] = m[i] - f * pivot_row
                for k in range(block):
                    diagonal = e[q][k] if diagonal is None else jnp.where(sub >= start + k, e[q][k], diagonal)
                    upper = jnp.where(lane == first + k, e[q][k], upper)
            scale = lax.rsqrt(diagonal)
            inside = (lane >= row) & (lane < row + 8)
            u_ref[:, row : row + 8, :] = jnp.where(
                lane >= sub + row, jnp.where(inside, upper, m[q]) * scale, 0.0
            )
            m_ref[:, row : row + 8, :] = jnp.where(lane <= sub + row, m[q] * scale, 0.0)
        after = base + group
        if after < width:
            lane_rest = iota((width - after, width), 1)
            lane_panel = iota((group, width), 1)
            for b in range(n):
                u = u_ref[b, base:after, :]
                right = jnp.where(lane_panel < after, m_ref[b, base:after, :], u)
                update = dot(u, right, ((0,), (0,)))
                old = m_ref[b, after:, :]
                old = jnp.where((lane_rest >= base) & (lane_rest < after), 0.0, old)
                m_ref[b, after:, :] = old - update[after:]


def vmem():
    return pl.BlockSpec(memory_space=pltpu.VMEM)


def shape(*dims):
    return jax.ShapeDtypeStruct(dims, jnp.float32)


PIECE = 32


def turned(value, pieces):
    shift = pieces * PIECE % value.shape[1]
    return pltpu.roll(value, shift, 1) if shift else value


def leaf_sample(index, offsets, near, panels, panel, nugget):
    parts, size, width = panels[0].shape
    split = size // 2

    def kernel(index_ref, offset_ref, near_ref, more_ref, *refs):
        panel_refs, (panel_ref, nugget_ref, sample_ref, gram_ref, packed_ref, buffer, sems) = refs[:3], refs[3:]
        for k in range(parts):
            offset = offset_ref[k]
            for part, ref in enumerate(panel_refs):

                @pl.when(offset // parts == part)
                def _():
                    pltpu.make_async_copy(ref.at[lax.rem(offset, parts)], buffer.at[k], sems.at[k]).start()

        row = nugget_ref[pl.ds(index_ref[1], 1), :]
        column = jnp.broadcast_to(row, (8, size)).T[:, :1]
        sample_ref[...] = column * panel_ref[0]
        for k in range(parts):
            pltpu.make_async_copy(panel_refs[0].at[0], buffer.at[k], sems.at[k]).wait()
            sample_ref[:split] += dot(near_ref[k, :split], buffer[k], ((1,), (0,)))
            sample_ref[split:] += dot(more_ref[k], buffer[k], ((1,), (0,)))
        half = width // 2
        gram_ref[...] = dot(sample_ref[:, :half], sample_ref[...], ((0,), (0,)))
        lane = iota((half, half), 1)
        for q in range(half // PIECE):
            gram = turned(gram_ref[:, :half], -q)
            cross = turned(gram_ref[:, half:], 1 - q)
            packed_ref[half * q : half * (q + 1)] = jnp.where(lane < PIECE, gram, cross)

    anywhere = pl.BlockSpec(memory_space=pl.ANY)
    smem = pl.BlockSpec(memory_space=pltpu.SMEM)
    return pl.pallas_call(
        kernel,
        in_specs=[smem, smem, vmem(), vmem()] + [anywhere] * 3 + [vmem()] * 2,
        out_specs=[vmem()] * 3,
        out_shape=[
            shape(size, width),
            shape(width // 2, width),
            shape(width // 2 * (width // 2 // PIECE), width // 2),
        ],
        scratch_shapes=[pltpu.VMEM((parts, size, width), jnp.float32), pltpu.SemaphoreType.DMA((parts,))],
        name="leaf_sample",
    )(index, offsets, *near, *panels, panel, nugget)


def node_children(leaf_count):
    level = [[i] for i in range(leaf_count)]
    nodes = []
    while len(level) > 1:
        pairs = [(level[2 * i], level[2 * i + 1]) for i in range(len(level) // 2)]
        nodes += pairs
        level = [a + b for a, b in pairs]
    return nodes


def tree_sums(pieces, leaf_count):
    total_leaves, width = pieces.shape
    count = total_leaves // leaf_count

    def kernel(pieces_ref, out_ref):
        rows = sum(pieces_ref[pl.ds(i, count, stride=leaf_count), :] for i in range(leaf_count))
        r = iota((count, count), 0)
        s = iota((count, count), 1)
        stride = r & -r
        root = r == 0
        left = root | ((s >= r - stride) & (s < r))
        right = (s >= r) & (s < r + stride)
        a = dot(jnp.where(left, 1.0, 0.0), rows, ((1,), (0,)))
        b = dot(jnp.where(right, 1.0, 0.0), rows, ((1,), (0,)))
        lane = iota((count, width), 1)
        root = iota((count, width), 0) == 0
        total = turned(a + b, 1)
        cross = turned(a, -1)
        for c in range(leaf_count):
            child = jnp.where(root, cross, a if c < leaf_count // 2 else b)
            out_ref[pl.ds(c, count, stride=leaf_count), :] = jnp.where(lane < PIECE, child, total)

    return pl.pallas_call(
        kernel, in_specs=[vmem()], out_specs=vmem(), out_shape=shape(total_leaves, width), name="tree_sums"
    )(pieces)


def local_bases(index, grams, gram, sample):
    parts = grams.shape[0]
    size, width = sample.shape
    half = width // 2
    share = width // parts
    nodes = node_children(parts)
    nodes = nodes + [nodes[-1]] * (parts - len(nodes))

    def kernel(index_ref, grams_ref, gram_ref, sample_ref, message_ref, m_ref, u_ref):
        column = index_ref[1]
        m_ref[0] = gram_ref[:, :half]
        for c, children in enumerate(nodes):

            @pl.when(column == c)
            def _():
                for side in range(2):
                    m_ref[1 + side] = sum(grams_ref[i, :, :half] for i in children[side])

        m_ref[3] = m_ref[1] + m_ref[2]
        factorize(m_ref, u_ref, 32, 8)
        inverse = m_ref[0]
        basis = dot(sample_ref[:, :half], inverse, ((1,), (1,)))
        reduced = dot(inverse, gram_ref[:, half:], ((1,), (0,)))
        missed = sample_ref[:, half:] - dot(basis, reduced, ((1,), (0,)))
        node_a = dot(u_ref[1], m_ref[3], ((1,), (1,)))
        node_b = dot(u_ref[2], m_ref[3], ((1,), (1,)))
        for c in range(parts):
            message_ref[c, 0] = basis[share * c : share * (c + 1)]
            message_ref[c, 1] = missed[share * c : share * (c + 1)]
            node = node_a if c < parts // 2 else node_b
            at = share * (c % (parts // 2))
            message_ref[c, 2] = node[at : at + share]

    return pl.pallas_call(
        kernel,
        in_specs=[pl.BlockSpec(memory_space=pltpu.SMEM), vmem(), vmem(), vmem()],
        out_specs=vmem(),
        out_shape=shape(parts, 3, share, half),
        scratch_shapes=[pltpu.VMEM((4, half, half), jnp.float32)] * 2,
        cost_estimate=pl.CostEstimate(flops=2 * 10**9, bytes_accessed=2 * 10**7, transcendentals=0),
        name="local_bases",
    )(index, grams, gram, sample)


def upper_share(index, received, root_scale, parts):
    half = received.shape[1]
    share = 2 * half // parts

    def kernel(index_ref, received_ref, upper_ref, m_ref, u_ref):
        lane = iota((half, half), 1)

        def assembled(t):
            value = turned(received_ref[:half], -t)
            for q in range(1, half // PIECE):
                piece = turned(received_ref[half * q : half * (q + 1)], q - t)
                value = jnp.where(lane < q * PIECE, value, piece)
            return value

        m_ref[0] = assembled(0)
        m_ref[1] = assembled(1)
        factorize(m_ref, u_ref, 32, 8)
        root = index_ref[0] == 0
        column = index_ref[1]
        at = pl.multiple_of(share * lax.rem(column, parts // 2), share)

        @pl.when(jnp.logical_not(root))
        def _():
            upper_ref[...] = dot(u_ref[0, pl.ds(at, share), :], m_ref[1], ((1,), (1,)))

        @pl.when(root)
        def _():
            reduced_root = dot(m_ref[1], assembled(0), ((1,), (0,)))
            u_ref[0] = jnp.where(column < parts // 2, u_ref[1], reduced_root).T * root_scale
            upper_ref[...] = u_ref[0, pl.ds(at, share), :]

    return pl.pallas_call(
        kernel,
        in_specs=[pl.BlockSpec(memory_space=pltpu.SMEM), vmem()],
        out_specs=vmem(),
        out_shape=shape(share, half),
        scratch_shapes=[pltpu.VMEM((2, half, half), jnp.float32)] * 2,
        cost_estimate=pl.CostEstimate(flops=10**9, bytes_accessed=10**7, transcendentals=0),
        name="upper_share",
    )(index, received)


def neighbours(block):
    count = lax.axis_size("row")
    forward = [(i, i + 1) for i in range(count - 1)]
    backward = [(i + 1, i) for i in range(count - 1)]
    return lax.ppermute(block, "row", forward), lax.ppermute(block, "row", backward)


def exchange(block, axis):
    return lax.all_to_all(block, axis, 0, 0, tiled=True)


def on_device(near_blocks, column_block, test_panels, nugget):
    leaf_count = near_blocks.shape[0]
    size = near_blocks.shape[2]
    half = test_panels.shape[2] // 2
    row_count = lax.axis_size("row")
    col_count = lax.axis_size("col")
    row_index = lax.axis_index("row")
    col_index = lax.axis_index("col")
    index = jnp.stack([row_index, col_index]).astype(jnp.int32)

    split = size // 2
    number = jnp.broadcast_to(column_block[:, :, None].astype(jnp.float32), (leaf_count, 8, size))
    near = exchange(jnp.concatenate([near_blocks[:, 0, :split], number], axis=1), "col")
    own = lax.all_gather(test_panels, "col", axis=0, tiled=True)
    rest, own = lax.optimization_barrier((near_blocks[:, 0, split:], own))
    low, high = neighbours(own)
    more = exchange(rest, "col")
    offsets = near[:, split, 0].astype(jnp.int32) - (row_index - 1) * leaf_count
    sample, gram, packed = leaf_sample(index, offsets, (near, more), (low, own, high), test_panels, nugget)

    pieces = exchange(packed, ("row", "col"))
    grams = lax.all_gather(gram, "col", axis=0)
    received = exchange(tree_sums(pieces, leaf_count), ("row", "col"))
    outputs = exchange(local_bases(index, grams, gram, sample), "col")
    root_scale = 1.0 / math.sqrt(leaf_count * row_count * size)
    upper = upper_share(index, received, root_scale, col_count)
    stored = (outputs[:, 0], outputs[:, 1], outputs[: col_count - 1, 2], upper[None])
    return tuple(jnp.swapaxes(output, 1, 2) for output in stored)


def solution(mesh):
    placed = (
        P("row", "col", None, None),
        P("row", "col"),
        P(("row", "col"), None, None),
        P("row", None),
    )
    return jax.shard_map(
        on_device,
        mesh=mesh,
        in_specs=placed,
        out_specs=(P("row", None, "col"),) * 4,
        check_vma=False,
    )
```

```python
import math

import jax
import jax.numpy as jnp
from jax import lax
from jax.experimental import pallas as pl
from jax.experimental.pallas import tpu as pltpu
from jax.sharding import PartitionSpec as P

HIGHEST = lax.Precision.HIGHEST


def dot(left, right, dims):
    return lax.dot_general(
        left, right, (dims, ((), ())), precision=HIGHEST, preferred_element_type=jnp.float32
    )


def iota(shape, dim):
    return lax.broadcasted_iota(jnp.int32, shape, dim)


def factorize(m_ref, u_ref, group, block):
    n, width, _ = m_ref.shape
    sub = iota((n, 8, width), 1)
    lane = iota((n, 8, width), 2)

    def spread(value):
        return jnp.broadcast_to(value, (n, 8, width))

    for base in range(0, width, group):
        count = group // 8
        m = [m_ref[:, base + 8 * q : base + 8 * q + 8, :] for q in range(count)]
        for q in range(count):
            row = base + 8 * q
            diagonal = None
            upper = m[q]
            for start in range(0, 8, block):
                first = row + start
                e = {
                    i: [spread(m[i][:, :, first + k : first + k + 1]) for k in range(block)]
                    for i in range(q, count)
                }
                inside = (lane >= first) & (lane < first + block)
                for i in range(q, count):
                    fill = jnp.where((lane - row) == sub, 1.0, 0.0) if i == q else 0.0
                    m[i] = jnp.where(inside, fill, m[i])
                for k in range(block):
                    s = start + k
                    inverse = 1.0 / spread(e[q][k][:, s : s + 1, :])
                    pivot_row = spread(m[q][:, s : s + 1, :])
                    pivot_e = [spread(e[q][j][:, s : s + 1, :]) for j in range(k + 1, block)]
                    for i in range(q, count):
                        f = e[i][k] * inverse
                        if i == q:
                            f = jnp.where(sub > s, f, 0.0)
                        for j in range(k + 1, block):
                            e[i][j] = e[i][j] - f * pivot_e[j - k - 1]
                        m[i] = m[i] - f * pivot_row
                for k in range(block):
                    diagonal = e[q][k] if diagonal is None else jnp.where(sub >= start + k, e[q][k], diagonal)
                    upper = jnp.where(lane == first + k, e[q][k], upper)
            scale = lax.rsqrt(diagonal)
            inside = (lane >= row) & (lane < row + 8)
            u_ref[:, row : row + 8, :] = jnp.where(
                lane >= sub + row, jnp.where(inside, upper, m[q]) * scale, 0.0
            )
            m_ref[:, row : row + 8, :] = jnp.where(lane <= sub + row, m[q] * scale, 0.0)
        after = base + group
        if after < width:
            lane_rest = iota((width - after, width), 1)
            lane_panel = iota((group, width), 1)
            for b in range(n):
                u = u_ref[b, base:after, :]
                right = jnp.where(lane_panel < after, m_ref[b, base:after, :], u)
                update = dot(u, right, ((0,), (0,)))
                old = m_ref[b, after:, :]
                old = jnp.where((lane_rest >= base) & (lane_rest < after), 0.0, old)
                m_ref[b, after:, :] = old - update[after:]


def vmem():
    return pl.BlockSpec(memory_space=pltpu.VMEM)


def shape(*dims):
    return jax.ShapeDtypeStruct(dims, jnp.float32)


PIECE = 32


def turned(value, pieces):
    shift = pieces * PIECE % value.shape[1]
    return pltpu.roll(value, shift, 1) if shift else value


def leaf_sample(index, offsets, near, panels, panel, nugget):
    parts, size, _ = near.shape
    width = panel.shape[2]

    def kernel(index_ref, offset_ref, near_ref, *refs):
        panel_refs, (panel_ref, nugget_ref, sample_ref, gram_ref, packed_ref, buffer, sems) = refs[:3], refs[3:]
        for k in range(parts):
            offset = offset_ref[k]
            for part, ref in enumerate(panel_refs):

                @pl.when(offset // parts == part)
                def _():
                    pltpu.make_async_copy(
                        ref.at[lax.rem(offset, parts), pl.ds(0, size)], buffer.at[k], sems.at[k]
                    ).start()

        row = nugget_ref[pl.ds(index_ref[1], 1), :]
        column = jnp.broadcast_to(row, (8, size)).T[:, :1]
        sample_ref[...] = column * panel_ref[0]
        for k in range(parts):
            pltpu.make_async_copy(panel_refs[0].at[0, pl.ds(0, size)], buffer.at[k], sems.at[k]).wait()
            sample_ref[...] += dot(near_ref[k], buffer[k], ((1,), (0,)))
        half = width // 2
        gram_ref[...] = dot(sample_ref[:, :half], sample_ref[...], ((0,), (0,)))
        lane = iota((half, half), 1)
        for q in range(half // PIECE):
            gram = turned(gram_ref[:, :half], -q)
            cross = turned(gram_ref[:, half:], 1 - q)
            packed_ref[half * q : half * (q + 1)] = jnp.where(lane < PIECE, gram, cross)

    anywhere = pl.BlockSpec(memory_space=pl.ANY)
    smem = pl.BlockSpec(memory_space=pltpu.SMEM)
    return pl.pallas_call(
        kernel,
        in_specs=[smem, smem, vmem()] + [anywhere] * 3 + [vmem()] * 2,
        out_specs=[vmem()] * 3,
        out_shape=[
            shape(size, width),
            shape(width // 2, width),
            shape(width // 2 * (width // 2 // PIECE), width // 2),
        ],
        scratch_shapes=[pltpu.VMEM((parts, size, width), jnp.float32), pltpu.SemaphoreType.DMA((parts,))],
        name="leaf_sample",
    )(index, offsets, near, *panels, panel, nugget)


def node_children(leaf_count):
    level = [[i] for i in range(leaf_count)]
    nodes = []
    while len(level) > 1:
        pairs = [(level[2 * i], level[2 * i + 1]) for i in range(len(level) // 2)]
        nodes += pairs
        level = [a + b for a, b in pairs]
    return nodes


def tree_sums(pieces, leaf_count):
    total_leaves, width = pieces.shape
    count = total_leaves // leaf_count

    def kernel(pieces_ref, out_ref):
        rows = sum(pieces_ref[pl.ds(i, count, stride=leaf_count), :] for i in range(leaf_count))
        r = iota((count, count), 0)
        s = iota((count, count), 1)
        stride = r & -r
        root = r == 0
        left = root | ((s >= r - stride) & (s < r))
        right = (s >= r) & (s < r + stride)
        a = dot(jnp.where(left, 1.0, 0.0), rows, ((1,), (0,)))
        b = dot(jnp.where(right, 1.0, 0.0), rows, ((1,), (0,)))
        lane = iota((count, width), 1)
        root = iota((count, width), 0) == 0
        total = turned(a + b, 1)
        cross = turned(a, -1)
        for c in range(leaf_count):
            child = jnp.where(root, cross, a if c < leaf_count // 2 else b)
            out_ref[pl.ds(c, count, stride=leaf_count), :] = jnp.where(lane < PIECE, child, total)

    return pl.pallas_call(
        kernel, in_specs=[vmem()], out_specs=vmem(), out_shape=shape(total_leaves, width), name="tree_sums"
    )(pieces)


def local_bases(index, grams, gram, sample):
    parts = grams.shape[0]
    size, width = sample.shape
    half = width // 2
    share = width // parts
    nodes = node_children(parts)
    nodes = nodes + [nodes[-1]] * (parts - len(nodes))

    def kernel(index_ref, grams_ref, gram_ref, sample_ref, message_ref, m_ref, u_ref):
        column = index_ref[1]
        m_ref[0] = gram_ref[:, :half]
        for c, children in enumerate(nodes):

            @pl.when(column == c)
            def _():
                for side in range(2):
                    m_ref[1 + side] = sum(grams_ref[i, :, :half] for i in children[side])

        m_ref[3] = m_ref[1] + m_ref[2]
        factorize(m_ref, u_ref, 32, 8)
        inverse = m_ref[0]
        basis = dot(sample_ref[:, :half], inverse, ((1,), (1,)))
        reduced = dot(inverse, gram_ref[:, half:], ((1,), (0,)))
        missed = sample_ref[:, half:] - dot(basis, reduced, ((1,), (0,)))
        node_a = dot(u_ref[1], m_ref[3], ((1,), (1,)))
        node_b = dot(u_ref[2], m_ref[3], ((1,), (1,)))
        for c in range(parts):
            message_ref[c, 0] = basis[share * c : share * (c + 1)]
            message_ref[c, 1] = missed[share * c : share * (c + 1)]
            node = node_a if c < parts // 2 else node_b
            at = share * (c % (parts // 2))
            message_ref[c, 2] = node[at : at + share]

    return pl.pallas_call(
        kernel,
        in_specs=[pl.BlockSpec(memory_space=pltpu.SMEM), vmem(), vmem(), vmem()],
        out_specs=vmem(),
        out_shape=shape(parts, 3, share, half),
        scratch_shapes=[pltpu.VMEM((4, half, half), jnp.float32)] * 2,
        cost_estimate=pl.CostEstimate(flops=2 * 10**9, bytes_accessed=2 * 10**7, transcendentals=0),
        name="local_bases",
    )(index, grams, gram, sample)


def upper_share(index, received, root_scale, parts):
    half = received.shape[1]
    share = 2 * half // parts

    def kernel(index_ref, received_ref, upper_ref, m_ref, u_ref):
        lane = iota((half, half), 1)

        def assembled(t):
            value = turned(received_ref[:half], -t)
            for q in range(1, half // PIECE):
                piece = turned(received_ref[half * q : half * (q + 1)], q - t)
                value = jnp.where(lane < q * PIECE, value, piece)
            return value

        m_ref[0] = assembled(0)
        m_ref[1] = assembled(1)
        factorize(m_ref, u_ref, 32, 8)
        root = index_ref[0] == 0
        column = index_ref[1]
        at = pl.multiple_of(share * lax.rem(column, parts // 2), share)

        @pl.when(jnp.logical_not(root))
        def _():
            upper_ref[...] = dot(u_ref[0, pl.ds(at, share), :], m_ref[1], ((1,), (1,)))

        @pl.when(root)
        def _():
            reduced_root = dot(m_ref[1], assembled(0), ((1,), (0,)))
            u_ref[0] = jnp.where(column < parts // 2, u_ref[1], reduced_root).T * root_scale
            upper_ref[...] = u_ref[0, pl.ds(at, share), :]

    return pl.pallas_call(
        kernel,
        in_specs=[pl.BlockSpec(memory_space=pltpu.SMEM), vmem()],
        out_specs=vmem(),
        out_shape=shape(share, half),
        scratch_shapes=[pltpu.VMEM((2, half, half), jnp.float32)] * 2,
        cost_estimate=pl.CostEstimate(flops=10**9, bytes_accessed=10**7, transcendentals=0),
        name="upper_share",
    )(index, received)


def neighbours(block):
    count = lax.axis_size("row")
    forward = [(i, i + 1) for i in range(count - 1)]
    backward = [(i + 1, i) for i in range(count - 1)]
    return lax.ppermute(block, "row", forward), lax.ppermute(block, "row", backward)


def exchange(block, axis):
    return lax.all_to_all(block, axis, 0, 0, tiled=True)


def on_device(near_blocks, column_block, test_panels, nugget):
    leaf_count = near_blocks.shape[0]
    size = near_blocks.shape[2]
    half = test_panels.shape[2] // 2
    row_count = lax.axis_size("row")
    col_count = lax.axis_size("col")
    row_index = lax.axis_index("row")
    col_index = lax.axis_index("col")
    index = jnp.stack([row_index, col_index]).astype(jnp.int32)

    numbers = column_block.reshape(1, 1, leaf_count).astype(jnp.float32)
    numbers = jnp.pad(numbers, ((0, 0), (0, 7), (0, 2 * half - leaf_count)))
    own = lax.all_gather(jnp.concatenate([test_panels, numbers], axis=1), "col", axis=0, tiled=True)
    near = exchange(near_blocks[:, 0], "col")
    low, high = neighbours(own)
    columns = lax.dynamic_slice(own, (0, size, col_index), (col_count, 1, 1)).reshape(-1)
    offsets = columns.astype(jnp.int32) - (row_index - 1) * leaf_count
    sample, gram, packed = leaf_sample(index, offsets, near, (low, own, high), test_panels, nugget)

    pieces = exchange(packed, ("row", "col"))
    grams = lax.all_gather(gram, "col", axis=0)
    received = exchange(tree_sums(pieces, leaf_count), ("row", "col"))
    outputs = exchange(local_bases(index, grams, gram, sample), "col")
    root_scale = 1.0 / math.sqrt(leaf_count * row_count * size)
    upper = upper_share(index, received, root_scale, col_count)
    stored = (outputs[:, 0], outputs[:, 1], outputs[: col_count - 1, 2], upper[None])
    return tuple(jnp.swapaxes(output, 1, 2) for output in stored)


def solution(mesh):
    placed = (
        P("row", "col", None, None),
        P("row", "col"),
        P(("row", "col"), None, None),
        P("row", None),
    )
    return jax.shard_map(
        on_device,
        mesh=mesh,
        in_specs=placed,
        out_specs=(P("row", None, "col"),) * 4,
        check_vma=False,
    )
```

```python
import math

import jax
import jax.numpy as jnp
from jax import lax
from jax.experimental import pallas as pl
from jax.experimental.pallas import tpu as pltpu
from jax.sharding import PartitionSpec as P


HIGHEST = lax.Precision.HIGHEST


def dot(left, right, dims):
    return lax.dot_general(
        left, right, (dims, ((), ())), precision=HIGHEST, preferred_element_type=jnp.float32
    )


def iota(shape, dim):
    return lax.broadcasted_iota(jnp.int32, shape, dim)


def factorize(m_ref, u_ref, group, block):
    n, width, _ = m_ref.shape
    sub = iota((n, 8, width), 1)
    lane = iota((n, 8, width), 2)

    def spread(value):
        return jnp.broadcast_to(value, (n, 8, width))

    for base in range(0, width, group):
        count = group // 8
        m = [m_ref[:, base + 8 * q : base + 8 * q + 8, :] for q in range(count)]
        for q in range(count):
            row = base + 8 * q
            diagonal = None
            upper = m[q]
            for start in range(0, 8, block):
                first = row + start
                e = {
                    i: [spread(m[i][:, :, first + k : first + k + 1]) for k in range(block)]
                    for i in range(q, count)
                }
                inside = (lane >= first) & (lane < first + block)
                for i in range(q, count):
                    fill = jnp.where((lane - row) == sub, 1.0, 0.0) if i == q else 0.0
                    m[i] = jnp.where(inside, fill, m[i])
                for k in range(block):
                    s = start + k
                    inverse = 1.0 / spread(e[q][k][:, s : s + 1, :])
                    pivot_row = spread(m[q][:, s : s + 1, :])
                    pivot_e = [spread(e[q][j][:, s : s + 1, :]) for j in range(k + 1, block)]
                    for i in range(q, count):
                        f = e[i][k] * inverse
                        if i == q:
                            f = jnp.where(sub > s, f, 0.0)
                        for j in range(k + 1, block):
                            e[i][j] = e[i][j] - f * pivot_e[j - k - 1]
                        m[i] = m[i] - f * pivot_row
                for k in range(block):
                    diagonal = e[q][k] if diagonal is None else jnp.where(sub >= start + k, e[q][k], diagonal)
                    upper = jnp.where(lane == first + k, e[q][k], upper)
            scale = lax.rsqrt(diagonal)
            inside = (lane >= row) & (lane < row + 8)
            u_ref[:, row : row + 8, :] = jnp.where(
                lane >= sub + row, jnp.where(inside, upper, m[q]) * scale, 0.0
            )
            m_ref[:, row : row + 8, :] = jnp.where(lane <= sub + row, m[q] * scale, 0.0)
        after = base + group
        if after < width:
            lane_rest = iota((width - after, width), 1)
            lane_panel = iota((group, width), 1)
            for b in range(n):
                u = u_ref[b, base:after, :]
                right = jnp.where(lane_panel < after, m_ref[b, base:after, :], u)
                update = dot(u, right, ((0,), (0,)))
                old = m_ref[b, after:, :]
                old = jnp.where((lane_rest >= base) & (lane_rest < after), 0.0, old)
                m_ref[b, after:, :] = old - update[after:]


def vmem():
    return pl.BlockSpec(memory_space=pltpu.VMEM)


def shape(*dims):
    return jax.ShapeDtypeStruct(dims, jnp.float32)


PIECE = 32
FIRST_ROWS = 104


def turned(value, pieces):
    shift = pieces * PIECE % value.shape[1]
    return pltpu.roll(value, shift, 1) if shift else value


def leaf_sample(index, offsets, near, panels, panel, nugget):
    parts, size, width = panels[0].shape
    split = FIRST_ROWS

    def kernel(index_ref, offset_ref, near_ref, more_ref, *refs):
        panel_refs, (panel_ref, nugget_ref, sample_ref, gram_ref, packed_ref, buffer, sems) = refs[:3], refs[3:]
        for k in range(parts):
            offset = offset_ref[k]
            for part, ref in enumerate(panel_refs):

                @pl.when(offset // parts == part)
                def _():
                    pltpu.make_async_copy(ref.at[lax.rem(offset, parts)], buffer.at[k], sems.at[k]).start()

        row = nugget_ref[pl.ds(index_ref[1], 1), :]
        column = jnp.broadcast_to(row, (8, size)).T[:, :1]
        sample_ref[...] = column * panel_ref[0]
        for k in range(parts):
            pltpu.make_async_copy(panel_refs[0].at[0], buffer.at[k], sems.at[k]).wait()
            sample_ref[:split] += dot(near_ref[k, :split], buffer[k], ((1,), (0,)))
            sample_ref[split:] += dot(more_ref[k], buffer[k], ((1,), (0,)))
        half = width // 2
        gram_ref[...] = dot(sample_ref[:, :half], sample_ref[...], ((0,), (0,)))
        lane = iota((half, half), 1)
        for q in range(half // PIECE):
            gram = turned(gram_ref[:, :half], -q)
            cross = turned(gram_ref[:, half:], 1 - q)
            packed_ref[half * q : half * (q + 1)] = jnp.where(lane < PIECE, gram, cross)

    anywhere = pl.BlockSpec(memory_space=pl.ANY)
    smem = pl.BlockSpec(memory_space=pltpu.SMEM)
    return pl.pallas_call(
        kernel,
        in_specs=[smem, smem, vmem(), vmem()] + [anywhere] * 3 + [vmem()] * 2,
        out_specs=[vmem()] * 3,
        out_shape=[
            shape(size, width),
            shape(width // 2, width),
            shape(width // 2 * (width // 2 // PIECE), width // 2),
        ],
        scratch_shapes=[pltpu.VMEM((parts, size, width), jnp.float32), pltpu.SemaphoreType.DMA((parts,))],
        name="leaf_sample",
    )(index, offsets, *near, *panels, panel, nugget)


def node_children(leaf_count):
    level = [[i] for i in range(leaf_count)]
    nodes = []
    while len(level) > 1:
        pairs = [(level[2 * i], level[2 * i + 1]) for i in range(len(level) // 2)]
        nodes += pairs
        level = [a + b for a, b in pairs]
    return nodes


def tree_sums(pieces, leaf_count):
    total_leaves, width = pieces.shape
    count = total_leaves // leaf_count

    def kernel(pieces_ref, out_ref):
        rows = sum(pieces_ref[pl.ds(i, count, stride=leaf_count), :] for i in range(leaf_count))
        r = iota((count, count), 0)
        s = iota((count, count), 1)
        stride = r & -r
        root = r == 0
        left = root | ((s >= r - stride) & (s < r))
        right = (s >= r) & (s < r + stride)
        a = dot(jnp.where(left, 1.0, 0.0), rows, ((1,), (0,)))
        b = dot(jnp.where(right, 1.0, 0.0), rows, ((1,), (0,)))
        lane = iota((count, width), 1)
        root = iota((count, width), 0) == 0
        total = turned(a + b, 1)
        cross = turned(a, -1)
        for c in range(leaf_count):
            child = jnp.where(root, cross, a if c < leaf_count // 2 else b)
            out_ref[pl.ds(c, count, stride=leaf_count), :] = jnp.where(lane < PIECE, child, total)

    return pl.pallas_call(
        kernel, in_specs=[vmem()], out_specs=vmem(), out_shape=shape(total_leaves, width), name="tree_sums"
    )(pieces)


def local_bases(index, grams, gram, sample):
    parts = grams.shape[0]
    _, width = sample.shape
    half = width // 2
    share = width // parts
    nodes = node_children(parts)
    nodes = nodes + [nodes[-1]] * (parts - len(nodes))

    def kernel(index_ref, grams_ref, gram_ref, sample_ref, message_ref, m_ref, u_ref):
        column = index_ref[1]
        m_ref[0] = gram_ref[:, :half]
        for c, children in enumerate(nodes):

            @pl.when(column == c)
            def _():
                for side in range(2):
                    m_ref[1 + side] = sum(grams_ref[i, :, :half] for i in children[side])

        m_ref[3] = m_ref[1] + m_ref[2]
        factorize(m_ref, u_ref, 32, 8)
        inverse = m_ref[0]
        basis = dot(sample_ref[:, :half], inverse, ((1,), (1,)))
        reduced = dot(inverse, gram_ref[:, half:], ((1,), (0,)))
        missed = sample_ref[:, half:] - dot(basis, reduced, ((1,), (0,)))
        node_a = dot(u_ref[1], m_ref[3], ((1,), (1,)))
        node_b = dot(u_ref[2], m_ref[3], ((1,), (1,)))
        for c in range(parts):
            message_ref[c, 0] = basis[share * c : share * (c + 1)]
            message_ref[c, 1] = missed[share * c : share * (c + 1)]
            node = node_a if c < parts // 2 else node_b
            at = share * (c % (parts // 2))
            message_ref[c, 2] = node[at : at + share]

    return pl.pallas_call(
        kernel,
        in_specs=[pl.BlockSpec(memory_space=pltpu.SMEM), vmem(), vmem(), vmem()],
        out_specs=vmem(),
        out_shape=shape(parts, 3, share, half),
        scratch_shapes=[pltpu.VMEM((4, half, half), jnp.float32)] * 2,
        cost_estimate=pl.CostEstimate(flops=2 * 10**9, bytes_accessed=2 * 10**7, transcendentals=0),
        name="local_bases",
    )(index, grams, gram, sample)


def upper_share(index, received, root_scale, parts):
    half = received.shape[1]
    share = 2 * half // parts

    def kernel(index_ref, received_ref, upper_ref, m_ref, u_ref):
        lane = iota((half, half), 1)

        def assembled(t):
            value = turned(received_ref[:half], -t)
            for q in range(1, half // PIECE):
                piece = turned(received_ref[half * q : half * (q + 1)], q - t)
                value = jnp.where(lane < q * PIECE, value, piece)
            return value

        m_ref[0] = assembled(0)
        m_ref[1] = assembled(1)
        factorize(m_ref, u_ref, 32, 8)
        root = index_ref[0] == 0
        column = index_ref[1]
        at = pl.multiple_of(share * lax.rem(column, parts // 2), share)

        @pl.when(jnp.logical_not(root))
        def _():
            upper_ref[...] = dot(u_ref[0, pl.ds(at, share), :], m_ref[1], ((1,), (1,)))

        @pl.when(root)
        def _():
            reduced_root = dot(m_ref[1], assembled(0), ((1,), (0,)))
            u_ref[0] = jnp.where(column < parts // 2, u_ref[1], reduced_root).T * root_scale
            upper_ref[...] = u_ref[0, pl.ds(at, share), :]

    return pl.pallas_call(
        kernel,
        in_specs=[pl.BlockSpec(memory_space=pltpu.SMEM), vmem()],
        out_specs=vmem(),
        out_shape=shape(share, half),
        scratch_shapes=[pltpu.VMEM((2, half, half), jnp.float32)] * 2,
        cost_estimate=pl.CostEstimate(flops=10**9, bytes_accessed=10**7, transcendentals=0),
        name="upper_share",
    )(index, received)


def neighbours(block):
    count = lax.axis_size("row")
    forward = [(i, i + 1) for i in range(count - 1)]
    backward = [(i + 1, i) for i in range(count - 1)]
    return lax.ppermute(block, "row", forward), lax.ppermute(block, "row", backward)


def exchange(block, axis):
    return lax.all_to_all(block, axis, 0, 0, tiled=True)


def on_device(near_blocks, column_block, test_panels, nugget):
    leaf_count = near_blocks.shape[0]
    size = near_blocks.shape[2]
    row_count = lax.axis_size("row")
    col_count = lax.axis_size("col")
    row_index = lax.axis_index("row")
    col_index = lax.axis_index("col")
    index = jnp.stack([row_index, col_index]).astype(jnp.int32)

    split = FIRST_ROWS
    number = jnp.broadcast_to(column_block[:, :, None].astype(jnp.float32), (leaf_count, 8, size))
    near = exchange(jnp.concatenate([near_blocks[:, 0, :split], number], axis=1), "col")
    own = lax.all_gather(test_panels, "col", axis=0, tiled=True)
    rest = near_blocks[:, 0, split:]
    rest, own = lax.optimization_barrier((rest, own))
    more = exchange(rest, "col")
    low, high = neighbours(own)
    offsets = near[:, split, 0].astype(jnp.int32) - (row_index - 1) * leaf_count
    sample, gram, packed = leaf_sample(index, offsets, (near, more), (low, own, high), test_panels, nugget)

    pieces = exchange(packed, ("row", "col"))
    grams = lax.all_gather(gram, "col", axis=0)
    received = exchange(tree_sums(pieces, leaf_count), ("row", "col"))
    outputs = exchange(local_bases(index, grams, gram, sample), "col")
    root_scale = 1.0 / math.sqrt(leaf_count * row_count * size)
    upper = upper_share(index, received, root_scale, col_count)
    stored = (outputs[:, 0], outputs[:, 1], outputs[: col_count - 1, 2], upper[None])
    return tuple(jnp.swapaxes(output, 1, 2) for output in stored)


def solution(mesh):
    placed = (
        P("row", "col", None, None),
        P("row", "col"),
        P(("row", "col"), None, None),
        P("row", None),
    )
    return jax.shard_map(
        on_device,
        mesh=mesh,
        in_specs=placed,
        out_specs=(P("row", None, "col"),) * 4,
        check_vma=False,
    )
```

```python
import math

import jax
import jax.numpy as jnp
from jax import lax
from jax.experimental import pallas as pl
from jax.experimental.pallas import tpu as pltpu
from jax.sharding import PartitionSpec as P


HIGHEST = lax.Precision.HIGHEST


def dot(left, right, dims):
    return lax.dot_general(
        left, right, (dims, ((), ())), precision=HIGHEST, preferred_element_type=jnp.float32
    )


def iota(shape, dim):
    return lax.broadcasted_iota(jnp.int32, shape, dim)


def factorize(m_ref, u_ref, group, block):
    n, width, _ = m_ref.shape
    sub = iota((n, 8, width), 1)
    lane = iota((n, 8, width), 2)

    def spread(value):
        return jnp.broadcast_to(value, (n, 8, width))

    for base in range(0, width, group):
        count = group // 8
        m = [m_ref[:, base + 8 * q : base + 8 * q + 8, :] for q in range(count)]
        for q in range(count):
            row = base + 8 * q
            diagonal = None
            upper = m[q]
            for start in range(0, 8, block):
                first = row + start
                e = {
                    i: [spread(m[i][:, :, first + k : first + k + 1]) for k in range(block)]
                    for i in range(q, count)
                }
                inside = (lane >= first) & (lane < first + block)
                for i in range(q, count):
                    fill = jnp.where((lane - row) == sub, 1.0, 0.0) if i == q else 0.0
                    m[i] = jnp.where(inside, fill, m[i])
                for k in range(block):
                    s = start + k
                    inverse = 1.0 / spread(e[q][k][:, s : s + 1, :])
                    pivot_row = spread(m[q][:, s : s + 1, :])
                    pivot_e = [spread(e[q][j][:, s : s + 1, :]) for j in range(k + 1, block)]
                    for i in range(q, count):
                        f = e[i][k] * inverse
                        if i == q:
                            f = jnp.where(sub > s, f, 0.0)
                        for j in range(k + 1, block):
                            e[i][j] = e[i][j] - f * pivot_e[j - k - 1]
                        m[i] = m[i] - f * pivot_row
                for k in range(block):
                    diagonal = e[q][k] if diagonal is None else jnp.where(sub >= start + k, e[q][k], diagonal)
                    upper = jnp.where(lane == first + k, e[q][k], upper)
            scale = lax.rsqrt(diagonal)
            inside = (lane >= row) & (lane < row + 8)
            u_ref[:, row : row + 8, :] = jnp.where(
                lane >= sub + row, jnp.where(inside, upper, m[q]) * scale, 0.0
            )
            m_ref[:, row : row + 8, :] = jnp.where(lane <= sub + row, m[q] * scale, 0.0)
        after = base + group
        if after < width:
            lane_rest = iota((width - after, width), 1)
            lane_panel = iota((group, width), 1)
            for b in range(n):
                u = u_ref[b, base:after, :]
                right = jnp.where(lane_panel < after, m_ref[b, base:after, :], u)
                update = dot(u, right, ((0,), (0,)))
                old = m_ref[b, after:, :]
                old = jnp.where((lane_rest >= base) & (lane_rest < after), 0.0, old)
                m_ref[b, after:, :] = old - update[after:]


def vmem():
    return pl.BlockSpec(memory_space=pltpu.VMEM)


def shape(*dims):
    return jax.ShapeDtypeStruct(dims, jnp.float32)


PIECE = 32
FIRST_ROWS = 104


def turned(value, pieces):
    shift = pieces * PIECE % value.shape[1]
    return pltpu.roll(value, shift, 1) if shift else value


def leaf_sample(index, offsets, near, panels, panel, nugget):
    parts, size, width = panels[0].shape
    split = FIRST_ROWS

    def kernel(index_ref, offset_ref, near_ref, more_ref, *refs):
        panel_refs, (panel_ref, nugget_ref, sample_ref, gram_ref, packed_ref, buffer, blocks, sems) = refs[:3], refs[3:]

        def block_copies(k):
            upper, lower = pl.ds(0, split), pl.ds(split, size - split)
            return (
                pltpu.make_async_copy(near_ref.at[k, upper], blocks.at[k, upper], sems.at[1, k]),
                pltpu.make_async_copy(more_ref.at[k], blocks.at[k, lower], sems.at[2, k]),
            )

        for k in range(parts):
            for copy in block_copies(k):
                copy.start()
            offset = offset_ref[k]
            for part, ref in enumerate(panel_refs):

                @pl.when(offset // parts == part)
                def _():
                    pltpu.make_async_copy(ref.at[lax.rem(offset, parts)], buffer.at[k], sems.at[0, k]).start()

        row = nugget_ref[pl.ds(index_ref[1], 1), :]
        column = jnp.broadcast_to(row, (8, size)).T[:, :1]
        sample_ref[...] = column * panel_ref[0]
        for k in range(parts):
            pltpu.make_async_copy(panel_refs[0].at[0], buffer.at[k], sems.at[0, k]).wait()
            for copy in block_copies(k):
                copy.wait()
            sample_ref[...] += dot(blocks[k], buffer[k], ((1,), (0,)))
        half = width // 2
        gram_ref[...] = dot(sample_ref[:, :half], sample_ref[...], ((0,), (0,)))
        lane = iota((half, half), 1)
        for q in range(half // PIECE):
            gram = turned(gram_ref[:, :half], -q)
            cross = turned(gram_ref[:, half:], 1 - q)
            packed_ref[half * q : half * (q + 1)] = jnp.where(lane < PIECE, gram, cross)

    anywhere = pl.BlockSpec(memory_space=pl.ANY)
    smem = pl.BlockSpec(memory_space=pltpu.SMEM)
    return pl.pallas_call(
        kernel,
        in_specs=[smem, smem, anywhere, anywhere] + [anywhere] * 3 + [vmem()] * 2,
        out_specs=[vmem()] * 3,
        out_shape=[
            shape(size, width),
            shape(width // 2, width),
            shape(width // 2 * (width // 2 // PIECE), width // 2),
        ],
        scratch_shapes=[
            pltpu.VMEM((parts, size, width), jnp.float32),
            pltpu.VMEM((parts, size, size), jnp.float32),
            pltpu.SemaphoreType.DMA((3, parts)),
        ],
        compiler_params=pltpu.CompilerParams(vmem_limit_bytes=16 * 2**20),
        name="leaf_sample",
    )(index, offsets, *near, *panels, panel, nugget)


def node_children(leaf_count):
    level = [[i] for i in range(leaf_count)]
    nodes = []
    while len(level) > 1:
        pairs = [(level[2 * i], level[2 * i + 1]) for i in range(len(level) // 2)]
        nodes += pairs
        level = [a + b for a, b in pairs]
    return nodes


def tree_sums(pieces, leaf_count):
    total_leaves, width = pieces.shape
    count = total_leaves // leaf_count

    def kernel(pieces_ref, out_ref):
        rows = sum(pieces_ref[pl.ds(i, count, stride=leaf_count), :] for i in range(leaf_count))
        r = iota((count, count), 0)
        s = iota((count, count), 1)
        stride = r & -r
        root = r == 0
        left = root | ((s >= r - stride) & (s < r))
        right = (s >= r) & (s < r + stride)
        a = dot(jnp.where(left, 1.0, 0.0), rows, ((1,), (0,)))
        b = dot(jnp.where(right, 1.0, 0.0), rows, ((1,), (0,)))
        lane = iota((count, width), 1)
        root = iota((count, width), 0) == 0
        total = turned(a + b, 1)
        cross = turned(a, -1)
        for c in range(leaf_count):
            child = jnp.where(root, cross, a if c < leaf_count // 2 else b)
            out_ref[pl.ds(c, count, stride=leaf_count), :] = jnp.where(lane < PIECE, child, total)

    return pl.pallas_call(
        kernel, in_specs=[vmem()], out_specs=vmem(), out_shape=shape(total_leaves, width), name="tree_sums"
    )(pieces)


def local_bases(index, grams, gram, sample):
    parts = grams.shape[0]
    _, width = sample.shape
    half = width // 2
    share = width // parts
    nodes = node_children(parts)
    nodes = nodes + [nodes[-1]] * (parts - len(nodes))

    def kernel(index_ref, grams_ref, gram_ref, sample_ref, message_ref, m_ref, u_ref):
        column = index_ref[1]
        m_ref[0] = gram_ref[:, :half]
        for c, children in enumerate(nodes):

            @pl.when(column == c)
            def _():
                for side in range(2):
                    m_ref[1 + side] = sum(grams_ref[i, :, :half] for i in children[side])

        m_ref[3] = m_ref[1] + m_ref[2]
        factorize(m_ref, u_ref, 32, 8)
        inverse = m_ref[0]
        basis = dot(sample_ref[:, :half], inverse, ((1,), (1,)))
        reduced = dot(inverse, gram_ref[:, half:], ((1,), (0,)))
        missed = sample_ref[:, half:] - dot(basis, reduced, ((1,), (0,)))
        node_a = dot(u_ref[1], m_ref[3], ((1,), (1,)))
        node_b = dot(u_ref[2], m_ref[3], ((1,), (1,)))
        for c in range(parts):
            message_ref[c, 0] = basis[share * c : share * (c + 1)]
            message_ref[c, 1] = missed[share * c : share * (c + 1)]
            node = node_a if c < parts // 2 else node_b
            at = share * (c % (parts // 2))
            message_ref[c, 2] = node[at : at + share]

    return pl.pallas_call(
        kernel,
        in_specs=[pl.BlockSpec(memory_space=pltpu.SMEM), vmem(), vmem(), vmem()],
        out_specs=vmem(),
        out_shape=shape(parts, 3, share, half),
        scratch_shapes=[pltpu.VMEM((4, half, half), jnp.float32)] * 2,
        cost_estimate=pl.CostEstimate(flops=2 * 10**9, bytes_accessed=2 * 10**7, transcendentals=0),
        name="local_bases",
    )(index, grams, gram, sample)


def upper_share(index, received, root_scale, parts):
    half = received.shape[1]
    share = 2 * half // parts

    def kernel(index_ref, received_ref, upper_ref, m_ref, u_ref):
        lane = iota((half, half), 1)

        def assembled(t):
            value = turned(received_ref[:half], -t)
            for q in range(1, half // PIECE):
                piece = turned(received_ref[half * q : half * (q + 1)], q - t)
                value = jnp.where(lane < q * PIECE, value, piece)
            return value

        m_ref[0] = assembled(0)
        m_ref[1] = assembled(1)
        factorize(m_ref, u_ref, 32, 8)
        root = index_ref[0] == 0
        column = index_ref[1]
        at = pl.multiple_of(share * lax.rem(column, parts // 2), share)

        @pl.when(jnp.logical_not(root))
        def _():
            upper_ref[...] = dot(u_ref[0, pl.ds(at, share), :], m_ref[1], ((1,), (1,)))

        @pl.when(root)
        def _():
            reduced_root = dot(m_ref[1], assembled(0), ((1,), (0,)))
            u_ref[0] = jnp.where(column < parts // 2, u_ref[1], reduced_root).T * root_scale
            upper_ref[...] = u_ref[0, pl.ds(at, share), :]

    return pl.pallas_call(
        kernel,
        in_specs=[pl.BlockSpec(memory_space=pltpu.SMEM), vmem()],
        out_specs=vmem(),
        out_shape=shape(share, half),
        scratch_shapes=[pltpu.VMEM((2, half, half), jnp.float32)] * 2,
        cost_estimate=pl.CostEstimate(flops=10**9, bytes_accessed=10**7, transcendentals=0),
        name="upper_share",
    )(index, received)


def neighbours(block):
    count = lax.axis_size("row")
    forward = [(i, i + 1) for i in range(count - 1)]
    backward = [(i + 1, i) for i in range(count - 1)]
    return lax.ppermute(block, "row", forward), lax.ppermute(block, "row", backward)


def exchange(block, axis):
    return lax.all_to_all(block, axis, 0, 0, tiled=True)


def on_device(near_blocks, column_block, test_panels, nugget):
    leaf_count = near_blocks.shape[0]
    size = near_blocks.shape[2]
    row_count = lax.axis_size("row")
    col_count = lax.axis_size("col")
    row_index = lax.axis_index("row")
    col_index = lax.axis_index("col")
    index = jnp.stack([row_index, col_index]).astype(jnp.int32)

    split = FIRST_ROWS
    number = jnp.broadcast_to(column_block[:, :, None].astype(jnp.float32), (leaf_count, 8, size))
    near = exchange(jnp.concatenate([near_blocks[:, 0, :split], number], axis=1), "col")
    own = lax.all_gather(test_panels, "col", axis=0, tiled=True)
    rest = near_blocks[:, 0, split:]
    rest, own = lax.optimization_barrier((rest, own))
    more = exchange(rest, "col")
    low, high = neighbours(own)
    offsets = near[:, split, 0].astype(jnp.int32) - (row_index - 1) * leaf_count
    sample, gram, packed = leaf_sample(index, offsets, (near, more), (low, own, high), test_panels, nugget)

    pieces = exchange(packed, ("row", "col"))
    grams = lax.all_gather(gram, "col", axis=0)
    received = exchange(tree_sums(pieces, leaf_count), ("row", "col"))
    outputs = exchange(local_bases(index, grams, gram, sample), "col")
    root_scale = 1.0 / math.sqrt(leaf_count * row_count * size)
    upper = upper_share(index, received, root_scale, col_count)
    stored = (outputs[:, 0], outputs[:, 1], outputs[: col_count - 1, 2], upper[None])
    return tuple(jnp.swapaxes(output, 1, 2) for output in stored)


def solution(mesh):
    placed = (
        P("row", "col", None, None),
        P("row", "col"),
        P(("row", "col"), None, None),
        P("row", None),
    )
    return jax.shard_map(
        on_device,
        mesh=mesh,
        in_specs=placed,
        out_specs=(P("row", None, "col"),) * 4,
        check_vma=False,
    )
```
